32 devices in a mesh: gz: 2 (over core), xy: 16 (over z, y, x).
Axes of the slice: x: 2, y: 2, z: 4, core: 2. Of those that a mesh axis runs over, the one named last changes fastest.
Arguments:
- state: float32 [64, 3, 7, 32768], P(('gz', 'xy')), may hold values from -4 to 4
- new_slot: int32 [64], P(('gz', 'xy')), may hold values from 0 to 63, as said below
- neighbor: int32 [64, 6], P(('gz', 'xy')), may hold values from -1 to 63, as said below
- stress: float32 [192, 128], P(('gz', 'xy')), may hold values from -6 to 6
- row_patch: int32 [192], P(('gz', 'xy')), may hold values from 0 to 63, as said below
Outputs:
- new_state: float32 [64, 7, 32768], P(('gz', 'xy'))
- velocity: float32 [64, 3, 32768], P(('gz', 'xy'))
The draws below stay inside these ranges and needn't reach their ends.
Inputs may be any that keep to these rules, and one draw needn't show every extreme that they name: `new_slot`: A permutation of the slots (slots d * 2 to d * 2 + 1 are held by device d = gz * 16 + xy). Every patch moves to a device with the same xy index; no device sends more than 1 of its patches to one device, so each device receives 2 patches from 2 different devices. `row_patch`: each row names a patch held by the same device as the row. A patch owns at most 4 rows, and on every device one patch owns exactly 4. `neighbor`: -1 on the domain boundary; else a slot held by the same device as the patch or by one of the two devices beside it in the order gz, xy (gz slowest).
All inputs are finite; a program needn't handle non-finite values.
Results may differ from the reference program's by a relative error of at most 0.000094.
Values sent between devices are 32-bit elements; how exact they have to be, the bound alone decides.
A program may use at most 256 MiB of HBM per device.

```python
import jax
import jax.numpy as jnp
from jax import lax

P_DEV = 2
EDGE = 32
SPECIES = 6
STRESS = 128
RMAX = 4
SWEEPS = 3
NPATCH = 64
NROW_DEV = 6
NROW = 192
N_GZ = 2
N_XY = 16


def draw_new_slot(key, part):

    def column_slots(column_key, column):
        keys = jax.random.split(column_key, 3)
        offsets = jax.random.permutation(keys[0], N_GZ)[:P_DEV]
        flips = jax.random.randint(keys[1], (N_GZ,), 0, P_DEV)
        swaps = jax.random.randint(keys[2], (N_GZ,), 0, P_DEV)
        source = jnp.arange(N_GZ)[:, None]
        within = jnp.arange(P_DEV)[None, :]
        order = (within + swaps[:, None]) % P_DEV
        target = (source + offsets[order]) % N_GZ
        new_local = (order + flips[target]) % P_DEV
        return ((target * N_XY + column) * P_DEV + new_local).astype(jnp.int32)
    column_keys = jax.vmap(lambda column: jax.random.fold_in(key, column))(jnp.arange(N_XY))
    slots = jax.vmap(column_slots)(column_keys, jnp.arange(N_XY))
    return jnp.transpose(slots, (1, 0, 2)).reshape(-1)


def draw_row_patch(key, part):

    def device_rows(device_key, device):
        keys = jax.random.split(device_key, 3)
        chosen = jax.random.permutation(keys[0], P_DEV)
        others = jax.random.permutation(keys[1], (P_DEV - 1) * RMAX)[:NROW_DEV - RMAX]
        slots = jnp.concatenate([jnp.full((RMAX,), chosen[0], jnp.int32), chosen[1 + others // RMAX].astype(jnp.int32)])
        slots = slots[jax.random.permutation(keys[2], NROW_DEV)]
        return (device * P_DEV + slots).astype(jnp.int32)
    devices = N_GZ * N_XY
    device_keys = jax.vmap(lambda device: jax.random.fold_in(key, device + 7))(jnp.arange(devices))
    return jax.vmap(device_rows)(device_keys, jnp.arange(devices)).reshape(-1)


def draw_neighbor(key, part):
    keys = jax.random.split(jax.random.fold_in(key, 11), 3)
    reach = jax.random.randint(keys[0], (NPATCH, 6), 1, P_DEV + 1)
    signs = jax.random.randint(keys[1], (NPATCH, 6), 0, 2) * 2 - 1
    boundary = jax.random.randint(keys[2], (NPATCH, 6), 0, 8) == 0
    target = jnp.arange(NPATCH)[:, None] + reach * signs
    valid = (target >= 0) & (target < NPATCH) & jnp.logical_not(boundary)
    return jnp.where(valid, target, -1).astype(jnp.int32)


def steps_of(own_key, shape, cuts, smallest, top_value):
    loudness, own = 1.0, jax.random.fold_in(own_key, 6)
    for position, blocks in cuts:
        steps = jnp.exp(jax.random.uniform(jax.random.fold_in(own, position), (blocks,), jnp.float32, smallest / len(cuts), top_value / len(cuts)))
        loudness = loudness * jnp.repeat(steps, shape[position] // blocks).reshape([-1 if axis == position else 1 for axis in range(len(shape))])
    return loudness


def normal_values(key, dims, spread, most, shards=(), kind=jnp.bfloat16):
    result = jax.random.normal(key, dims, jnp.float32) * spread
    if len(shards) > 0:
        result = steps_of(key, dims, shards, -0.22, 0.18) * result
    return jnp.clip(result, min=-most, max=most).astype(kind)


def setup_inputs(seed: int = 0) -> dict:
    splits = jax.random.split(jax.random.key(seed), 6)
    return {
        "state": normal_values(splits[0], (NPATCH, 3, SPECIES + 1, EDGE ** 3), 0.3, 4.0, ((0, 32),), jnp.float32),
        "new_slot": draw_new_slot(jax.random.fold_in(splits[5], 71), 0),
        "neighbor": draw_neighbor(jax.random.fold_in(splits[5], 71), 0),
        "stress": normal_values(splits[3], (NROW, STRESS), 2.0, 6.0, ((0, 32),), jnp.float32),
        "row_patch": draw_row_patch(jax.random.fold_in(splits[5], 71), 0),
    }


OPPOSITE = (1, 0, 3, 2, 5, 4)
viscous_rate = 0.3
surface_tension = 0.5
drag_factor = 1.0
gradient_energy = 0.5
mobility = 0.2
time_step = 0.02
half_saturation = 0.5


def combine(levels):
    current = levels[:, 0]
    previous = levels[:, 1]
    earlier = levels[:, 2]
    extrap = 3.0 * current - 3.0 * previous + earlier
    history = (18.0 * current - 9.0 * previous + 2.0 * earlier) / 11.0
    return extrap, history


def face_stack(field):
    patches, components = field.shape[0], field.shape[1]
    cells_grid = field.reshape(patches, components, EDGE, EDGE, EDGE)
    surfaces = [cells_grid[:, :, 0], cells_grid[:, :, -1], cells_grid[:, :, :, 0], cells_grid[:, :, :, -1], cells_grid[:, :, :, :, 0], cells_grid[:, :, :, :, -1]]
    return jnp.stack([s.reshape(patches, components, EDGE * EDGE) for s in surfaces], axis=1)


def neighbours(field, ghosts):
    patches, components = field.shape[0], field.shape[1]
    grid = field.reshape(patches, components, EDGE, EDGE, EDGE)

    def plane(face):
        return ghosts[:, face].reshape(patches, components, EDGE, EDGE)

    lower_x = jnp.concatenate([plane(0)[:, :, None], grid[:, :, :-1]], axis=2)
    upper_x = jnp.concatenate([grid[:, :, 1:], plane(1)[:, :, None]], axis=2)
    lower_y = jnp.concatenate([plane(2)[:, :, :, None], grid[:, :, :, :-1]], axis=3)
    upper_y = jnp.concatenate([grid[:, :, :, 1:], plane(3)[:, :, :, None]], axis=3)
    lower_z = jnp.concatenate([plane(4)[..., None], grid[..., :-1]], axis=4)
    upper_z = jnp.concatenate([grid[..., 1:], plane(5)[..., None]], axis=4)
    return grid, [lower_x, upper_x, lower_y, upper_y, lower_z, upper_z]


def terms(extrap, ghosts, totals):
    patches = extrap.shape[0]
    center, nearby = neighbours(extrap, ghosts)
    laplace = nearby[0] + nearby[1] + nearby[2] + nearby[3] + nearby[4] + nearby[5] - 6.0 * center
    gradient = [(nearby[1] - nearby[0]) * 0.5, (nearby[3] - nearby[2]) * 0.5, (nearby[5] - nearby[4]) * 0.5]
    phase = center[:, 0]
    viscous = jnp.exp(viscous_rate * phase)
    face_visc = [(viscous + jnp.exp(viscous_rate * n[:, 0])) * 0.5 for n in nearby]
    diagonal = drag_factor * viscous + face_visc[0] + face_visc[1] + face_visc[2] + face_visc[3] + face_visc[4] + face_visc[5]
    row_lines = totals.shape[1] // EDGE
    traction = totals.reshape(patches, 1, row_lines, EDGE)
    traction = jnp.pad(traction, ((0, 0), (0, EDGE - 1), (0, EDGE - row_lines), (0, 0)))
    forcing = jnp.stack([surface_tension * phase * gradient[0][:, 0] + traction, surface_tension * phase * gradient[1][:, 0], surface_tension * phase * gradient[2][:, 0]], axis=1)
    return center, laplace, gradient, phase, face_visc, diagonal, forcing


def start_velocity(forcing, diagonal):
    patches = forcing.shape[0]
    return (forcing / diagonal[:, None]).reshape(patches, 3, -1)


def sweep(velocity, ghosts, face_visc, diagonal, forcing):
    patches = velocity.shape[0]
    vel_near = neighbours(velocity, ghosts)[1]
    coupled = face_visc[0][:, None] * vel_near[0]
    for face in range(1, 6):
        coupled = coupled + face_visc[face][:, None] * vel_near[face]
    return ((forcing + coupled) / diagonal[:, None]).reshape(patches, 3, -1)


def potential_of(phase, laplace):
    patches = phase.shape[0]
    potential = phase * phase * phase - phase - gradient_energy * laplace[:, 0]
    return potential.reshape(patches, 1, -1)


def finish(history, center, laplace, gradient, phase, velocity, potential, pot_ghosts):
    patches = history.shape[0]
    diffusion = jnp.array([0.8, 1.0, 0.6, 1.2, 0.9, 0.7], jnp.float32).reshape(1, 6, 1, 1, 1)
    growth = jnp.array([1.0, 0.5, 2.0, 1.5, 0.8, 1.2], jnp.float32).reshape(1, 6, 1, 1, 1)
    pot_center, pot_near = neighbours(potential, pot_ghosts)
    pot_laplace = pot_near[0] + pot_near[1] + pot_near[2] + pot_near[3] + pot_near[4] + pot_near[5] - 6.0 * pot_center
    grid_vel = velocity.reshape(patches, 3, EDGE, EDGE, EDGE)
    advect = grid_vel[:, 0:1] * gradient[0] + grid_vel[:, 1:2] * gradient[1] + grid_vel[:, 2:3] * gradient[2]
    phase_rate = mobility * pot_laplace[:, 0] - advect[:, 0]
    biofilm = 0.5 * (1.0 + jnp.tanh(phase))
    species = center[:, 1:]
    uptake = growth * biofilm[:, None] * species / (half_saturation + jnp.abs(species))
    species_rate = diffusion * laplace[:, 1:] - advect[:, 1:] - uptake
    tendency = jnp.concatenate([phase_rate[:, None], species_rate], axis=1)
    return history + (6.0 / 11.0) * time_step * tendency.reshape(patches, 7, -1)


def reference(state, new_slot, neighbor, stress, row_patch):
    block = min(NPATCH, 4 * P_DEV)
    count = NPATCH // block

    def blocked(x):
        return x.reshape((count, block) + x.shape[1:])

    def whole(x):
        return x.reshape((NPATCH,) + x.shape[2:])

    inverse = jnp.zeros((NPATCH,), jnp.int32).at[new_slot].set(jnp.arange(NPATCH, dtype=jnp.int32))
    totals = jax.ops.segment_sum(stress, row_patch, num_segments=NPATCH)
    moved_totals = totals[inverse]
    moved_extrap = whole(lax.map(lambda index: combine(state[index])[0], blocked(inverse)))

    def ghost_fill(field):
        table = face_stack(field)
        pieces = []
        for face in range(6):
            picked = table[jnp.clip(neighbor[:, face], 0, NPATCH - 1), OPPOSITE[face]]
            pieces.append(jnp.where(neighbor[:, face, None, None] >= 0, picked, 0.0))
        return jnp.stack(pieces, axis=1)

    extrap_ghosts = ghost_fill(moved_extrap)
    base = (blocked(moved_extrap), blocked(extrap_ghosts), blocked(moved_totals))

    def first(args):
        parts = terms(args[0], args[1], args[2])
        return start_velocity(parts[6], parts[5])

    velocity = whole(lax.map(first, base))
    for sweep_index in range(SWEEPS - 1):
        vel_ghosts = ghost_fill(velocity)

        def again(args):
            parts = terms(args[0], args[1], args[2])
            return sweep(args[3], args[4], parts[4], parts[5], parts[6])

        velocity = whole(lax.map(again, base + (blocked(velocity), blocked(vel_ghosts))))

    def pot_section(args):
        parts = terms(args[0], args[1], args[2])
        return potential_of(parts[3], parts[1])

    potential = whole(lax.map(pot_section, base))
    pot_ghosts = ghost_fill(potential)

    def last(args):
        parts = terms(args[0], args[1], args[2])
        history = combine(state[args[3]])[1]
        return finish(history, parts[0], parts[1], parts[2], parts[3], args[4], args[5], args[6])

    new_state = whole(lax.map(last, base + (blocked(inverse), blocked(velocity), blocked(potential), blocked(pot_ghosts))))
    return new_state, velocity
```

```python
import jax
import jax.numpy as jnp
from jax import lax
from jax.experimental import pallas as pl
from jax.experimental.pallas import tpu as pltpu
from jax.sharding import PartitionSpec as P

EDGE = 32
CELLS = EDGE**3
FIELDS = 7
OPPOSITE = (1, 0, 3, 2, 5, 4)
DIFFUSION = (0.8, 1.0, 0.6, 1.2, 0.9, 0.7)
GROWTH = (1.0, 0.5, 2.0, 1.5, 0.8, 1.2)
RATE = 6.0 / 11.0 * 0.02
CHUNKS = 4
MESH = pl.DeviceIdType.MESH


def iota(axis):
    return lax.broadcasted_iota(jnp.int32, (8, 128), axis)


def roll(v, shift, axis):
    if isinstance(shift, int) and shift % v.shape[axis] == 0:
        return v
    if isinstance(shift, int):
        shift = shift % v.shape[axis]
    return pltpu.roll(v, shift, axis)


def rows(start):
    return pl.ds(start if isinstance(start, int) else pl.multiple_of(start, 8), 8)


def pack(block, slot, fields, table, first, count):
    pitch = fields * 8
    lane = iota(1)
    own = (2 + slot) * 6
    table[own] = block[pl.ds(pitch + first * 8, count * 8), :]
    table[own + 1] = block[pl.ds(EDGE * pitch + first * 8, count * 8), :]
    for f in range(count):
        low = high = None
        for j in range(4):
            at = (8 * j + 1) * pitch + (first + f) * 8
            a = roll(block[pl.ds(at, 8, stride=pitch), :], 32 * j, 1)
            b = roll(block[pl.ds(at + 7, 8, stride=pitch), :], 32 * j + 32, 1)
            low = a if j == 0 else jnp.where(lane // 32 == j, a, low)
            high = b if j == 0 else jnp.where(lane // 32 == j, b, high)
        table[own + 2, pl.ds(f * 8, 8)] = low
        table[own + 3, pl.ds(f * 8, 8)] = high

    for f in range(count):
        low = high = None
        for x in range(EDGE):
            v = roll(block[pl.ds((x + 1) * pitch + (first + f) * 8, 8), :], x, 1)
            low = v if x == 0 else jnp.where(lane % 32 == x, v, low)
            high = v if x == 0 else jnp.where(lane % 32 == x - 1, v, high)
        table[own + 4, pl.ds(f * 8, 8)] = low
        table[own + 5, pl.ds(f * 8, 8)] = roll(high, 97, 1)


def fill(block, slot, fields, table, neighbor, lower, y_ghost, z_ghost, first, count):
    pitch = fields * 8
    for face in range(6):
        beyond = neighbor[slot, face]
        inside = beyond >= 0
        pick = jnp.where(inside, jnp.clip(beyond - lower, 0, 5), 2) * 6 + OPPOSITE[face]
        tile = jnp.where(inside, table[pick], 0.0)
        if face == 0:
            block[pl.ds(first * 8, count * 8), :] = tile
        elif face == 1:
            block[pl.ds((EDGE + 1) * pitch + first * 8, count * 8), :] = tile
        elif face < 4:
            for f in range(count):
                one = tile[f * 8 : f * 8 + 8]
                for j in range(4):
                    shift = -32 * j if face == 2 else 96 - 32 * j
                    y_ghost[face - 2, pl.ds(f * 32 + j * 8, 8)] = roll(one, shift, 1)
        else:
            z_ghost[face - 4] = tile


def nearby(block, fields, f, x, y_ghost, z_ghost, first=0):
    pitch = fields * 8
    lane, sub = iota(1), iota(0)
    at = (x + 1) * pitch + f * 8
    v = block[rows(at), :]
    f = f - first
    y_low = y_ghost[0, pl.ds(f * 32 + x, 1)]
    y_high = y_ghost[1, pl.ds(f * 32 + x, 1)]
    down = roll(v, 32, 1)
    up = roll(v, 96, 1)
    lower_y = jnp.where(lane < 32, jnp.where(sub == 0, y_low, roll(down, 1, 0)), down)
    upper_y = jnp.where(lane >= 96, jnp.where(sub == 7, y_high, roll(up, 7, 0)), up)
    z_low = roll(z_ghost[0, pl.ds(f * 8, 8)], 128 - x, 1)
    z_high = roll(z_ghost[1, pl.ds(f * 8, 8)], 31 - x + 128, 1)
    lower_z = jnp.where(lane % 32 == 0, z_low, roll(v, 1, 1))
    upper_z = jnp.where(lane % 32 == 31, z_high, roll(v, 127, 1))
    return v, (block[rows(at - pitch), :], block[rows(at + pitch), :], lower_y, upper_y, lower_z, upper_z)


def total(parts):
    return ((parts[0] + parts[1]) + (parts[2] + parts[3])) + (parts[4] + parts[5])


def make_kernel(columns, devices):
    def kernel(
        state, new_slot_in, neighbor_in, stress_in, row_patch_in, out_state, out_velocity,
        levels, send_e, send_h, stay_e, came_e, stay_h, came_h,
        cells, table_p, table_a, table_b, table_2, table_3,
        yg_p, zg_p, yg_a, zg_a, yg_b, zg_b, yg_2, zg_2, yg_3, zg_3,
        first, second, weight, force, slope, base, full_state, full_velocity,
        new_slot, neighbor, row_patch, stress, small_sem, load_sem, send_sem, recv_sem, face_send, face_recv, store_sem,
    ):
        gz, xy = lax.axis_index("gz"), lax.axis_index("xy")
        device = gz * columns + xy
        left, right = device - 1, device + 1
        lower = (device - 1) * 2

        def place(d):
            return (d // columns, d % columns)

        width = EDGE * 16 // CHUNKS
        loads = []
        for c in range(CHUNKS):
            part = pl.ds(c * width, width)
            loads.append(
                pltpu.make_async_copy(state.at[:, :, part], levels.at[:, :, part], load_sem.at[c])
            )
            loads[-1].start()

        small = []
        for k, (a, b) in enumerate(
            ((new_slot_in, new_slot), (neighbor_in, neighbor), (row_patch_in, row_patch), (stress_in, stress))
        ):
            small.append(pltpu.make_async_copy(a, b, small_sem.at[k]))
            small[-1].start()

        barrier = pltpu.get_barrier_semaphore()
        pl.semaphore_signal(barrier, inc=1, device_id=(1 - gz, xy), device_id_type=MESH)

        @pl.when(device > 0)
        def _():
            pl.semaphore_signal(barrier, inc=1, device_id=place(left), device_id_type=MESH)

        @pl.when(device < devices - 1)
        def _():
            pl.semaphore_signal(barrier, inc=1, device_id=place(right), device_id_type=MESH)

        @pl.when(device > 1)
        def _():
            pl.semaphore_signal(barrier, inc=1, device_id=place(device - 2), device_id_type=MESH)

        @pl.when(device < devices - 2)
        def _():
            pl.semaphore_signal(barrier, inc=1, device_id=place(device + 2), device_id_type=MESH)

        below = (device + devices - 1) // devices + (device + devices - 2) // devices
        above = (2 * devices - 2 - device) // devices + (2 * devices - 3 - device) // devices
        pl.semaphore_wait(barrier, 1 + below + above)

        for copy in small:
            copy.wait()
        start = device * 2
        zero_stays = (new_slot[0] >= start) & (new_slot[0] < start + 2)
        stay_slot = jnp.where(zero_stays, new_slot[0], new_slot[1]) - start

        sums = []
        for p in range(2):
            line = jnp.zeros((1, 128), jnp.float32)
            for r in range(stress.shape[0]):
                line = line + jnp.where(row_patch[r] == start + p, stress[r : r + 1, :], 0.0)
            sums.append(line)
        top = iota(0) == 0
        send_e[pl.ds(EDGE * 56, 8), :] = jnp.where(top, jnp.where(zero_stays, sums[1], sums[0]), 0.0)
        stay_e[pl.ds(EDGE * 56, 8), :] = jnp.where(top, jnp.where(zero_stays, sums[0], sums[1]), 0.0)

        def move(source, target, first_row, count, k):
            return pltpu.make_async_remote_copy(
                src_ref=source.at[pl.ds(first_row, count)],
                dst_ref=target.at[pl.ds(first_row, count)],
                send_sem=send_sem.at[k],
                recv_sem=recv_sem.at[k],
                device_id=(1 - gz, xy),
                device_id_type=MESH,
            )

        planes = EDGE // CHUNKS
        extrap_moves, history_moves = [], []
        for c in range(CHUNKS):
            loads[c].wait()

            def combine(x, carry):
                for f in range(FIELDS):
                    to = rows((x * FIELDS + f) * 8)
                    both = []
                    for p in range(2):
                        part = pl.ds(x * 16 + p, 8, stride=2)
                        a, b, d = (levels.at[k, f][part, :] for k in range(3))
                        both.append(
                            (3.0 * a - 3.0 * b + d, (18.0 * a - 9.0 * b + 2.0 * d) * (1.0 / 11.0))
                        )
                    send_e[to, :] = jnp.where(zero_stays, both[1][0], both[0][0])
                    stay_e[to, :] = jnp.where(zero_stays, both[0][0], both[1][0])
                    send_h[to, :] = jnp.where(zero_stays, both[1][1], both[0][1])
                    stay_h[to, :] = jnp.where(zero_stays, both[0][1], both[1][1])
                return carry

            lax.fori_loop(c * planes, (c + 1) * planes, combine, 0, unroll=2)
            count = planes * 56
            extra = 8 if c == CHUNKS - 1 else 0
            extrap_moves.append(move(send_e, came_e, c * count, count + extra, c))
            extrap_moves[-1].start()
        for c in range(CHUNKS):
            count = planes * 56
            history_moves.append(move(send_h, came_h, c * count, count, CHUNKS + c))
            history_moves[-1].start()

        stays = [stay_slot == s for s in range(2)]
        for c in range(CHUNKS):
            extrap_moves[c].wait_recv()

            def arrange(x, carry):
                part = pl.ds(pl.multiple_of(x * 56, 8), 56)
                to = pl.ds(pl.multiple_of((x + 1) * 56, 8), 56)
                here, there = stay_e[part, :], came_e[part, :]
                cells.at[0][to, :] = jnp.where(stays[0], here, there)
                cells.at[1][to, :] = jnp.where(stays[1], here, there)
                return carry

            lax.fori_loop(c * planes, (c + 1) * planes, arrange, 0)

        def faces(table, side, k):
            to, target = (0, right) if side == 0 else (24, left)
            return pltpu.make_async_remote_copy(
                src_ref=table.at[pl.ds(12, 12)],
                dst_ref=table.at[pl.ds(to, 12)],
                send_sem=face_send.at[2 * k + side],
                recv_sem=face_recv.at[2 * k + side],
                device_id=place(target),
                device_id_type=MESH,
            )

        def send_faces(table, k):
            @pl.when(device < devices - 1)
            def _():
                faces(table, 0, k).start()

            @pl.when(device > 0)
            def _():
                faces(table, 1, k).start()

        def await_faces(table, k):
            @pl.when(device > 0)
            def _():
                faces(table, 0, k).wait_recv()

            @pl.when(device < devices - 1)
            def _():
                faces(table, 1, k).wait_recv()

        odd = device % 2 == 1
        even = device % 2 == 0

        def hop(table, source, to, target, k):
            return pltpu.make_async_remote_copy(
                src_ref=table.at[pl.ds(source, 12)],
                dst_ref=table.at[pl.ds(to, 12)],
                send_sem=face_send.at[k],
                recv_sem=face_recv.at[k],
                device_id=place(target),
                device_id_type=MESH,
            )

        def to_partner(table, k, act):
            @pl.when(even)
            def _():
                act(hop(table, 12, 0, right, 2 * k))

            @pl.when(odd)
            def _():
                act(hop(table, 12, 24, left, 2 * k))

        def to_second(table, k, act):
            @pl.when(even & (device < devices - 2))
            def _():
                act(hop(table, 24, 0, device + 2, 2 * k + 1))

            @pl.when(odd & (device > 1))
            def _():
                act(hop(table, 0, 24, device - 2, 2 * k + 1))

        def hand_on(table, k):
            @pl.when(even)
            def _():
                hop(table, 12, 24, right, 2 * k).wait_recv()

            @pl.when(odd)
            def _():
                hop(table, 12, 0, left, 2 * k).wait_recv()

            to_second(table, k, lambda copy: copy.start())

        def await_second(table, k):
            @pl.when(even & (device > 0))
            def _():
                hop(table, 24, 0, device - 2, 2 * k + 1).wait_recv()

            @pl.when(odd & (device < devices - 1))
            def _():
                hop(table, 0, 24, device + 2, 2 * k + 1).wait_recv()

        groups = ((0, 1, table_p, yg_p, zg_p), (1, 3, table_a, yg_a, zg_a), (4, 3, table_b, yg_b, zg_b))

        def pack_cells(g):
            first_field, count, table = groups[g][:3]
            for s in range(2):
                pack(cells.at[s], s, FIELDS, table, first_field, count)

        def fill_cells(g):
            first_field, count, table, yg, zg = groups[g]
            for s in range(2):
                fill(
                    cells.at[s], s, FIELDS, table, neighbor, lower, yg.at[s], zg.at[s],
                    first_field, count,
                )

        pack_cells(0)
        send_faces(table_p, 0)
        pack_cells(1)
        to_partner(table_a, 1, lambda copy: copy.start())
        await_faces(table_p, 0)
        fill_cells(0)

        lines = pl.ds(EDGE * 56, 8)
        traction = [jnp.where(stays[s], stay_e[lines, :], came_e[lines, :]) for s in range(2)]

        def begin(x, carry):
            for s in range(2):
                v, near = nearby(cells.at[s], FIELDS, 0, x, yg_p.at[s], zg_p.at[s])
                viscous = jnp.exp(0.3 * v)
                sides = [(viscous + jnp.exp(0.3 * n)) * 0.5 for n in near]
                inverse = 1.0 / (viscous + total(sides))
                half = 0.25 * v
                for i in range(6):
                    weight.at[s][rows((x * 6 + i) * 8), :] = sides[i] * inverse
                for k in range(3):
                    f = half * (near[2 * k + 1] - near[2 * k])
                    if k == 0:
                        f = f + jnp.where(x == 0, traction[s], 0.0)
                    f = f * inverse
                    force.at[s][rows((x * 3 + k) * 8), :] = f
                    first.at[s][rows(((x + 1) * 4 + k) * 8), :] = f
                laplace = total(near) - 6.0 * v
                first.at[s][rows(((x + 1) * 4 + 3) * 8), :] = v * v * v - v - 0.5 * laplace
            return carry

        lax.fori_loop(0, EDGE, begin, 0, unroll=4)
        hand_on(table_a, 1)
        for s in range(2):
            pack(first.at[s], s, 4, table_2, 0, 4)
        send_faces(table_2, 3)
        pack_cells(2)
        to_partner(table_b, 2, lambda copy: copy.start())

        for c in range(CHUNKS):
            history_moves[c].wait_recv()

        def species(g):
            first_field, count, _, yg, zg = groups[g]

            def step(x, carry):
                for s in range(2):
                    if g > 0:
                        phi = cells.at[s][rows((x + 1) * 56), :]
                        biofilm = 0.5 * (1.0 + jnp.tanh(phi))
                    for f in range(first_field, first_field + count):
                        at = rows((x * 7 + f) * 8)
                        v, near = nearby(cells.at[s], FIELDS, f, x, yg.at[s], zg.at[s], first_field)
                        for k in range(3):
                            slope.at[s][rows(((x * 7 + f) * 3 + k) * 8), :] = (
                                near[2 * k + 1] - near[2 * k]
                            ) * (0.5 * RATE)
                        history = jnp.where(stays[s], stay_h[at, :], came_h[at, :])
                        if f > 0:
                            laplace = total(near) - 6.0 * v
                            uptake = GROWTH[f - 1] * biofilm * v / (0.5 + jnp.abs(v))
                            history = history + RATE * (DIFFUSION[f - 1] * laplace - uptake)
                        base.at[s][at, :] = history
                return carry

            lax.fori_loop(0, EDGE, step, 0, unroll=2)

        species(0)
        await_second(table_a, 1)
        fill_cells(1)
        species(1)
        await_faces(table_2, 3)
        for s in range(2):
            fill(first.at[s], s, 4, table_2, neighbor, lower, yg_2.at[s], zg_2.at[s], 0, 4)

        def sweep(block, fields, s, x, y_ghost, z_ghost):
            sides = [weight.at[s][rows((x * 6 + i) * 8), :] for i in range(6)]
            result = []
            for k in range(3):
                near = nearby(block.at[s], fields, k, x, y_ghost.at[s], z_ghost.at[s])[1]
                coupled = total([sides[i] * near[i] for i in range(6)])
                result.append(force.at[s][rows((x * 3 + k) * 8), :] + coupled)
            return result

        def again(x, carry):
            for s in range(2):
                velocity = sweep(first, 4, s, x, yg_2, zg_2)
                for k in range(3):
                    second.at[s][rows(((x + 1) * 3 + k) * 8), :] = velocity[k]
            return carry

        lax.fori_loop(0, EDGE, again, 0, unroll=4)
        hand_on(table_b, 2)
        for s in range(2):
            pack(second.at[s], s, 3, table_3, 0, 3)
        send_faces(table_3, 4)

        def phase(x, carry):
            for s in range(2):
                v, near = nearby(first.at[s], 4, 3, x, yg_2.at[s], zg_2.at[s])
                at = rows(x * 56)
                base.at[s][at, :] = base.at[s][at, :] + (0.2 * RATE) * (total(near) - 6.0 * v)
            return carry

        lax.fori_loop(0, EDGE, phase, 0, unroll=4)
        await_second(table_b, 2)
        fill_cells(2)
        species(2)
        await_faces(table_3, 4)
        for s in range(2):
            fill(second.at[s], s, 3, table_3, neighbor, lower, yg_3.at[s], zg_3.at[s], 0, 3)

        stores = []
        for c in range(CHUNKS):

            def finish(x, carry):
                for s in range(2):
                    velocity = sweep(second, 3, s, x, yg_3, zg_3)
                    to = pl.ds(x * 16 + s, 8, stride=2)
                    for k in range(3):
                        full_velocity.at[k][to, :] = velocity[k]
                    for f in range(FIELDS):
                        advect = [
                            velocity[k] * slope.at[s][rows(((x * 7 + f) * 3 + k) * 8), :]
                            for k in range(3)
                        ]
                        kept = base.at[s][rows((x * 7 + f) * 8), :]
                        full_state.at[f][to, :] = kept - (advect[0] + advect[1] + advect[2])
                return carry

            lax.fori_loop(c * planes, (c + 1) * planes, finish, 0, unroll=4)
            part = pl.ds(c * width, width)
            stores.append(
                pltpu.make_async_copy(full_state.at[:, part], out_state.at[:, part], store_sem.at[2 * c])
            )
            stores.append(
                pltpu.make_async_copy(
                    full_velocity.at[:, part], out_velocity.at[:, part], store_sem.at[2 * c + 1]
                )
            )
            stores[-2].start()
            stores[-1].start()

        for copy in extrap_moves + history_moves:
            copy.wait_send()
        for k, table in ((0, table_p), (3, table_2), (4, table_3)):

            @pl.when(device < devices - 1)
            def _():
                faces(table, 0, k).wait_send()

            @pl.when(device > 0)
            def _():
                faces(table, 1, k).wait_send()

        for k, table in ((1, table_a), (2, table_b)):
            to_partner(table, k, lambda copy: copy.wait_send())
            to_second(table, k, lambda copy: copy.wait_send())

        for copy in stores:
            copy.wait()

    return kernel


def on_device(state, new_slot, neighbor, stress, row_patch):
    peers, columns = lax.axis_size("gz"), lax.axis_size("xy")
    assert peers == 2 and state.shape == (2, 3, FIELDS, CELLS)
    f32 = jnp.float32

    def vmem(*shape):
        return pltpu.VMEM(shape, f32)

    size = EDGE * 56
    scratch = [vmem(3, FIELDS, EDGE * 16, 128)]
    scratch += [vmem(size + 8, 128), vmem(size, 128)]
    scratch += [vmem(size + 8, 128), vmem(size + 8, 128), vmem(size, 128), vmem(size, 128)]
    scratch += [vmem(2, size + 112, 128)]
    scratch += [vmem(36, c * 8, 128) for c in (1, 3, 3, 4, 3)]
    for c in (1, 3, 3, 4, 3):
        scratch += [vmem(2, 2, c * 32, 128), vmem(2, 2, c * 8, 128)]
    scratch += [vmem(2, 34 * 32, 128), vmem(2, 34 * 24, 128)]
    scratch += [vmem(2, EDGE * 48, 128), vmem(2, EDGE * 24, 128), vmem(2, EDGE * 168, 128)]
    scratch += [vmem(2, size, 128)]
    scratch += [vmem(FIELDS, EDGE * 16, 128), vmem(3, EDGE * 16, 128)]
    dma = pltpu.SemaphoreType.DMA
    small = ((new_slot, pltpu.SMEM), (neighbor, pltpu.SMEM), (row_patch, pltpu.SMEM), (stress, pltpu.VMEM))
    scratch += [space(a.shape, a.dtype) for a, space in small]
    scratch += [dma((4,)), dma((CHUNKS,)), dma((2 * CHUNKS,)), dma((2 * CHUNKS,)), dma((10,)), dma((10,)), dma((2 * CHUNKS,))]
    woven = state.reshape(2, 3, FIELDS, EDGE * 8, 128).transpose(1, 2, 3, 0, 4)
    outs = pl.pallas_call(
        make_kernel(columns, peers * columns),
        out_shape=(
            jax.ShapeDtypeStruct((FIELDS, EDGE * 16, 128), f32),
            jax.ShapeDtypeStruct((3, EDGE * 16, 128), f32),
        ),
        in_specs=[pl.BlockSpec(memory_space=pltpu.HBM)] * 5,
        out_specs=(pl.BlockSpec(memory_space=pltpu.HBM), pl.BlockSpec(memory_space=pltpu.HBM)),
        scratch_shapes=scratch,
        compiler_params=pltpu.CompilerParams(
            collective_id=0, has_side_effects=True, vmem_limit_bytes=64 * 2**20
        ),
    )(woven.reshape(3, FIELDS, EDGE * 16, 128), new_slot, neighbor, stress, row_patch)
    return tuple(
        out.reshape(-1, EDGE * 8, 2, 128).transpose(2, 0, 1, 3).reshape(2, -1, CELLS) for out in outs
    )


def solution(mesh):
    both = ("gz", "xy")
    in_specs = (P(both, None, None, None), P(both), P(both, None), P(both, None), P(both))
    out_specs = (P(both, None, None), P(both, None, None))
    return jax.shard_map(
        on_device, mesh=mesh, in_specs=in_specs, out_specs=out_specs, check_vma=False
    )
```

```python
import jax
import jax.numpy as jnp
from jax import lax
from jax.experimental import pallas as pl
from jax.experimental.pallas import tpu as pltpu
from jax.sharding import PartitionSpec as P

EDGE = 32
CELLS = EDGE**3
FIELDS = 7
OPPOSITE = (1, 0, 3, 2, 5, 4)
DIFFUSION = (0.8, 1.0, 0.6, 1.2, 0.9, 0.7)
GROWTH = (1.0, 0.5, 2.0, 1.5, 0.8, 1.2)
RATE = 6.0 / 11.0 * 0.02
CHUNKS = 4
MESH = pl.DeviceIdType.MESH


def iota(axis):
    return lax.broadcasted_iota(jnp.int32, (8, 128), axis)


def roll(v, shift, axis):
    if isinstance(shift, int) and shift % v.shape[axis] == 0:
        return v
    if isinstance(shift, int):
        shift = shift % v.shape[axis]
    return pltpu.roll(v, shift, axis)


def rows(start):
    return pl.ds(start if isinstance(start, int) else pl.multiple_of(start, 8), 8)


def pack(block, slot, fields, table, first, count):
    pitch = fields * 8
    lane = iota(1)
    own = (2 + slot) * 6
    table[own] = block[pl.ds(pitch + first * 8, count * 8), :]
    table[own + 1] = block[pl.ds(EDGE * pitch + first * 8, count * 8), :]
    for f in range(count):
        low = high = None
        for j in range(4):
            at = (8 * j + 1) * pitch + (first + f) * 8
            a = roll(block[pl.ds(at, 8, stride=pitch), :], 32 * j, 1)
            b = roll(block[pl.ds(at + 7, 8, stride=pitch), :], 32 * j + 32, 1)
            low = a if j == 0 else jnp.where(lane // 32 == j, a, low)
            high = b if j == 0 else jnp.where(lane // 32 == j, b, high)
        table[own + 2, pl.ds(f * 8, 8)] = low
        table[own + 3, pl.ds(f * 8, 8)] = high

    for f in range(count):
        low = high = None
        for x in range(EDGE):
            v = roll(block[pl.ds((x + 1) * pitch + (first + f) * 8, 8), :], x, 1)
            low = v if x == 0 else jnp.where(lane % 32 == x, v, low)
            high = v if x == 0 else jnp.where(lane % 32 == x - 1, v, high)
        table[own + 4, pl.ds(f * 8, 8)] = low
        table[own + 5, pl.ds(f * 8, 8)] = roll(high, 97, 1)


def fill(block, slot, fields, table, neighbor, lower, y_ghost, z_ghost, first, count):
    pitch = fields * 8
    for face in range(6):
        beyond = neighbor[slot, face]
        inside = beyond >= 0
        pick = jnp.where(inside, jnp.clip(beyond - lower, 0, 5), 2) * 6 + OPPOSITE[face]
        tile = jnp.where(inside, table[pick], 0.0)
        if face == 0:
            block[pl.ds(first * 8, count * 8), :] = tile
        elif face == 1:
            block[pl.ds((EDGE + 1) * pitch + first * 8, count * 8), :] = tile
        elif face < 4:
            for f in range(count):
                one = tile[f * 8 : f * 8 + 8]
                for j in range(4):
                    shift = -32 * j if face == 2 else 96 - 32 * j
                    y_ghost[face - 2, pl.ds(f * 32 + j * 8, 8)] = roll(one, shift, 1)
        else:
            z_ghost[face - 4] = tile


def nearby(block, fields, f, x, y_ghost, z_ghost, first=0):
    pitch = fields * 8
    lane, sub = iota(1), iota(0)
    at = (x + 1) * pitch + f * 8
    v = block[rows(at), :]
    f = f - first
    y_low = y_ghost[0, pl.ds(f * 32 + x, 1)]
    y_high = y_ghost[1, pl.ds(f * 32 + x, 1)]
    down = roll(v, 32, 1)
    up = roll(v, 96, 1)
    lower_y = jnp.where(lane < 32, jnp.where(sub == 0, y_low, roll(down, 1, 0)), down)
    upper_y = jnp.where(lane >= 96, jnp.where(sub == 7, y_high, roll(up, 7, 0)), up)
    z_low = roll(z_ghost[0, pl.ds(f * 8, 8)], 128 - x, 1)
    z_high = roll(z_ghost[1, pl.ds(f * 8, 8)], 31 - x + 128, 1)
    lower_z = jnp.where(lane % 32 == 0, z_low, roll(v, 1, 1))
    upper_z = jnp.where(lane % 32 == 31, z_high, roll(v, 127, 1))
    return v, (block[rows(at - pitch), :], block[rows(at + pitch), :], lower_y, upper_y, lower_z, upper_z)


def total(parts):
    return ((parts[0] + parts[1]) + (parts[2] + parts[3])) + (parts[4] + parts[5])


def make_kernel(columns, devices):
    def kernel(
        state, new_slot_in, neighbor_in, stress_in, row_patch_in, full_state, full_velocity,
        levels, send_e, send_h, stay_e, came_e, stay_h, came_h,
        cells, table_p, table_a, table_b, table_2, table_3,
        yg_p, zg_p, yg_a, zg_a, yg_b, zg_b, yg_2, zg_2, yg_3, zg_3,
        first, second, weight, force, slope, base,
        new_slot, neighbor, row_patch, stress, small_sem, load_sem, send_sem, recv_sem, face_send, face_recv,
    ):
        gz, xy = lax.axis_index("gz"), lax.axis_index("xy")
        device = gz * columns + xy
        left, right = device - 1, device + 1
        lower = (device - 1) * 2

        def place(d):
            return (d // columns, d % columns)

        width = EDGE * 16 // CHUNKS
        loads = []
        for c in range(CHUNKS):
            part = pl.ds(c * width, width)
            loads.append(
                pltpu.make_async_copy(state.at[:, :, part], levels.at[:, :, part], load_sem.at[c])
            )
            loads[-1].start()

        small = []
        for k, (a, b) in enumerate(
            ((new_slot_in, new_slot), (neighbor_in, neighbor), (row_patch_in, row_patch), (stress_in, stress))
        ):
            small.append(pltpu.make_async_copy(a, b, small_sem.at[k]))
            small[-1].start()

        barrier = pltpu.get_barrier_semaphore()
        pl.semaphore_signal(barrier, inc=1, device_id=(1 - gz, xy), device_id_type=MESH)

        @pl.when(device > 0)
        def _():
            pl.semaphore_signal(barrier, inc=1, device_id=place(left), device_id_type=MESH)

        @pl.when(device < devices - 1)
        def _():
            pl.semaphore_signal(barrier, inc=1, device_id=place(right), device_id_type=MESH)

        @pl.when(device > 1)
        def _():
            pl.semaphore_signal(barrier, inc=1, device_id=place(device - 2), device_id_type=MESH)

        @pl.when(device < devices - 2)
        def _():
            pl.semaphore_signal(barrier, inc=1, device_id=place(device + 2), device_id_type=MESH)

        below = (device + devices - 1) // devices + (device + devices - 2) // devices
        above = (2 * devices - 2 - device) // devices + (2 * devices - 3 - device) // devices
        pl.semaphore_wait(barrier, 1 + below + above)

        for copy in small:
            copy.wait()
        start = device * 2
        zero_stays = (new_slot[0] >= start) & (new_slot[0] < start + 2)
        stay_slot = jnp.where(zero_stays, new_slot[0], new_slot[1]) - start

        sums = []
        for p in range(2):
            line = jnp.zeros((1, 128), jnp.float32)
            for r in range(stress.shape[0]):
                line = line + jnp.where(row_patch[r] == start + p, stress[r : r + 1, :], 0.0)
            sums.append(line)
        top = iota(0) == 0
        send_e[pl.ds(EDGE * 56, 8), :] = jnp.where(top, jnp.where(zero_stays, sums[1], sums[0]), 0.0)
        stay_e[pl.ds(EDGE * 56, 8), :] = jnp.where(top, jnp.where(zero_stays, sums[0], sums[1]), 0.0)

        def move(source, target, first_row, count, k):
            return pltpu.make_async_remote_copy(
                src_ref=source.at[pl.ds(first_row, count)],
                dst_ref=target.at[pl.ds(first_row, count)],
                send_sem=send_sem.at[k],
                recv_sem=recv_sem.at[k],
                device_id=(1 - gz, xy),
                device_id_type=MESH,
            )

        planes = EDGE // CHUNKS
        extrap_moves, history_moves = [], []
        for c in range(CHUNKS):
            loads[c].wait()

            def combine(x, carry):
                for f in range(FIELDS):
                    to = rows((x * FIELDS + f) * 8)
                    both = []
                    for p in range(2):
                        part = pl.ds(x * 16 + p, 8, stride=2)
                        a, b, d = (levels.at[k, f][part, :] for k in range(3))
                        both.append(
                            (3.0 * a - 3.0 * b + d, (18.0 * a - 9.0 * b + 2.0 * d) * (1.0 / 11.0))
                        )
                    send_e[to, :] = jnp.where(zero_stays, both[1][0], both[0][0])
                    stay_e[to, :] = jnp.where(zero_stays, both[0][0], both[1][0])
                    send_h[to, :] = jnp.where(zero_stays, both[1][1], both[0][1])
                    stay_h[to, :] = jnp.where(zero_stays, both[0][1], both[1][1])
                return carry

            lax.fori_loop(c * planes, (c + 1) * planes, combine, 0, unroll=2)
            count = planes * 56
            extra = 8 if c == CHUNKS - 1 else 0
            extrap_moves.append(move(send_e, came_e, c * count, count + extra, c))
            extrap_moves[-1].start()
        for c in range(CHUNKS):
            count = planes * 56
            history_moves.append(move(send_h, came_h, c * count, count, CHUNKS + c))
            history_moves[-1].start()

        stays = [stay_slot == s for s in range(2)]
        for c in range(CHUNKS):
            extrap_moves[c].wait_recv()

            def arrange(x, carry):
                part = pl.ds(pl.multiple_of(x * 56, 8), 56)
                to = pl.ds(pl.multiple_of((x + 1) * 56, 8), 56)
                here, there = stay_e[part, :], came_e[part, :]
                cells.at[0][to, :] = jnp.where(stays[0], here, there)
                cells.at[1][to, :] = jnp.where(stays[1], here, there)
                return carry

            lax.fori_loop(c * planes, (c + 1) * planes, arrange, 0)

        def faces(table, side, k):
            to, target = (0, right) if side == 0 else (24, left)
            return pltpu.make_async_remote_copy(
                src_ref=table.at[pl.ds(12, 12)],
                dst_ref=table.at[pl.ds(to, 12)],
                send_sem=face_send.at[2 * k + side],
                recv_sem=face_recv.at[2 * k + side],
                device_id=place(target),
                device_id_type=MESH,
            )

        def send_faces(table, k):
            @pl.when(device < devices - 1)
            def _():
                faces(table, 0, k).start()

            @pl.when(device > 0)
            def _():
                faces(table, 1, k).start()

        def await_faces(table, k):
            @pl.when(device > 0)
            def _():
                faces(table, 0, k).wait_recv()

            @pl.when(device < devices - 1)
            def _():
                faces(table, 1, k).wait_recv()

        odd = device % 2 == 1
        even = device % 2 == 0

        def hop(table, source, to, target, k):
            return pltpu.make_async_remote_copy(
                src_ref=table.at[pl.ds(source, 12)],
                dst_ref=table.at[pl.ds(to, 12)],
                send_sem=face_send.at[k],
                recv_sem=face_recv.at[k],
                device_id=place(target),
                device_id_type=MESH,
            )

        def to_partner(table, k, act):
            @pl.when(even)
            def _():
                act(hop(table, 12, 0, right, 2 * k))

            @pl.when(odd)
            def _():
                act(hop(table, 12, 24, left, 2 * k))

        def to_second(table, k, act):
            @pl.when(even & (device < devices - 2))
            def _():
                act(hop(table, 24, 0, device + 2, 2 * k + 1))

            @pl.when(odd & (device > 1))
            def _():
                act(hop(table, 0, 24, device - 2, 2 * k + 1))

        def hand_on(table, k):
            @pl.when(even)
            def _():
                hop(table, 12, 24, right, 2 * k).wait_recv()

            @pl.when(odd)
            def _():
                hop(table, 12, 0, left, 2 * k).wait_recv()

            to_second(table, k, lambda copy: copy.start())

        def await_second(table, k):
            @pl.when(even & (device > 0))
            def _():
                hop(table, 24, 0, device - 2, 2 * k + 1).wait_recv()

            @pl.when(odd & (device < devices - 1))
            def _():
                hop(table, 0, 24, device + 2, 2 * k + 1).wait_recv()

        groups = ((0, 1, table_p, yg_p, zg_p), (1, 3, table_a, yg_a, zg_a), (4, 3, table_b, yg_b, zg_b))

        def pack_cells(g):
            first_field, count, table = groups[g][:3]
            for s in range(2):
                pack(cells.at[s], s, FIELDS, table, first_field, count)

        def fill_cells(g):
            first_field, count, table, yg, zg = groups[g]
            for s in range(2):
                fill(
                    cells.at[s], s, FIELDS, table, neighbor, lower, yg.at[s], zg.at[s],
                    first_field, count,
                )

        pack_cells(0)
        send_faces(table_p, 0)
        pack_cells(1)
        to_partner(table_a, 1, lambda copy: copy.start())
        await_faces(table_p, 0)
        fill_cells(0)

        lines = pl.ds(EDGE * 56, 8)
        traction = [jnp.where(stays[s], stay_e[lines, :], came_e[lines, :]) for s in range(2)]

        def begin(x, carry):
            for s in range(2):
                v, near = nearby(cells.at[s], FIELDS, 0, x, yg_p.at[s], zg_p.at[s])
                viscous = jnp.exp(0.3 * v)
                sides = [(viscous + jnp.exp(0.3 * n)) * 0.5 for n in near]
                inverse = 1.0 / (viscous + total(sides))
                half = 0.25 * v
                for i in range(6):
                    weight.at[s][rows((x * 6 + i) * 8), :] = sides[i] * inverse
                for k in range(3):
                    f = half * (near[2 * k + 1] - near[2 * k])
                    if k == 0:
                        f = f + jnp.where(x == 0, traction[s], 0.0)
                    f = f * inverse
                    force.at[s][rows((x * 3 + k) * 8), :] = f
                    first.at[s][rows(((x + 1) * 4 + k) * 8), :] = f
                laplace = total(near) - 6.0 * v
                first.at[s][rows(((x + 1) * 4 + 3) * 8), :] = v * v * v - v - 0.5 * laplace
            return carry

        lax.fori_loop(0, EDGE, begin, 0, unroll=4)
        hand_on(table_a, 1)
        for s in range(2):
            pack(first.at[s], s, 4, table_2, 0, 4)
        send_faces(table_2, 3)
        pack_cells(2)
        to_partner(table_b, 2, lambda copy: copy.start())

        for c in range(CHUNKS):
            history_moves[c].wait_recv()

        def species(g):
            first_field, count, _, yg, zg = groups[g]

            def step(x, carry):
                for s in range(2):
                    if g > 0:
                        phi = cells.at[s][rows((x + 1) * 56), :]
                        biofilm = 0.5 * (1.0 + jnp.tanh(phi))
                    for f in range(first_field, first_field + count):
                        at = rows((x * 7 + f) * 8)
                        v, near = nearby(cells.at[s], FIELDS, f, x, yg.at[s], zg.at[s], first_field)
                        for k in range(3):
                            slope.at[s][rows(((x * 7 + f) * 3 + k) * 8), :] = (
                                near[2 * k + 1] - near[2 * k]
                            ) * (0.5 * RATE)
                        history = jnp.where(stays[s], stay_h[at, :], came_h[at, :])
                        if f > 0:
                            laplace = total(near) - 6.0 * v
                            uptake = GROWTH[f - 1] * biofilm * v / (0.5 + jnp.abs(v))
                            history = history + RATE * (DIFFUSION[f - 1] * laplace - uptake)
                        base.at[s][at, :] = history
                return carry

            lax.fori_loop(0, EDGE, step, 0, unroll=2)

        species(0)
        await_second(table_a, 1)
        fill_cells(1)
        species(1)
        await_faces(table_2, 3)
        for s in range(2):
            fill(first.at[s], s, 4, table_2, neighbor, lower, yg_2.at[s], zg_2.at[s], 0, 4)

        def sweep(block, fields, s, x, y_ghost, z_ghost):
            sides = [weight.at[s][rows((x * 6 + i) * 8), :] for i in range(6)]
            result = []
            for k in range(3):
                near = nearby(block.at[s], fields, k, x, y_ghost.at[s], z_ghost.at[s])[1]
                coupled = total([sides[i] * near[i] for i in range(6)])
                result.append(force.at[s][rows((x * 3 + k) * 8), :] + coupled)
            return result

        def again(x, carry):
            for s in range(2):
                velocity = sweep(first, 4, s, x, yg_2, zg_2)
                for k in range(3):
                    second.at[s][rows(((x + 1) * 3 + k) * 8), :] = velocity[k]
            return carry

        lax.fori_loop(0, EDGE, again, 0, unroll=4)
        hand_on(table_b, 2)
        for s in range(2):
            pack(second.at[s], s, 3, table_3, 0, 3)
        send_faces(table_3, 4)

        def phase(x, carry):
            for s in range(2):
                v, near = nearby(first.at[s], 4, 3, x, yg_2.at[s], zg_2.at[s])
                at = rows(x * 56)
                base.at[s][at, :] = base.at[s][at, :] + (0.2 * RATE) * (total(near) - 6.0 * v)
            return carry

        lax.fori_loop(0, EDGE, phase, 0, unroll=4)
        await_second(table_b, 2)
        fill_cells(2)
        species(2)
        await_faces(table_3, 4)
        for s in range(2):
            fill(second.at[s], s, 3, table_3, neighbor, lower, yg_3.at[s], zg_3.at[s], 0, 3)

        for c in range(CHUNKS):

            def finish(x, carry):
                for s in range(2):
                    velocity = sweep(second, 3, s, x, yg_3, zg_3)
                    to = pl.ds(x * 16 + s, 8, stride=2)
                    for k in range(3):
                        full_velocity.at[k][to, :] = velocity[k]
                    for f in range(FIELDS):
                        advect = [
                            velocity[k] * slope.at[s][rows(((x * 7 + f) * 3 + k) * 8), :]
                            for k in range(3)
                        ]
                        kept = base.at[s][rows((x * 7 + f) * 8), :]
                        full_state.at[f][to, :] = kept - (advect[0] + advect[1] + advect[2])
                return carry

            lax.fori_loop(c * planes, (c + 1) * planes, finish, 0, unroll=4)
        for copy in extrap_moves + history_moves:
            copy.wait_send()
        for k, table in ((0, table_p), (3, table_2), (4, table_3)):

            @pl.when(device < devices - 1)
            def _():
                faces(table, 0, k).wait_send()

            @pl.when(device > 0)
            def _():
                faces(table, 1, k).wait_send()

        for k, table in ((1, table_a), (2, table_b)):
            to_partner(table, k, lambda copy: copy.wait_send())
            to_second(table, k, lambda copy: copy.wait_send())


    return kernel


def put_out(state, velocity, out_state, out_velocity, sem):
    copies = [
        pltpu.make_async_copy(state, out_state, sem.at[0]),
        pltpu.make_async_copy(velocity, out_velocity, sem.at[1]),
    ]
    for copy in copies:
        copy.start()
    for copy in copies:
        copy.wait()


def on_device(state, new_slot, neighbor, stress, row_patch):
    peers, columns = lax.axis_size("gz"), lax.axis_size("xy")
    assert peers == 2 and state.shape == (2, 3, FIELDS, CELLS)
    f32 = jnp.float32

    def vmem(*shape):
        return pltpu.VMEM(shape, f32)

    size = EDGE * 56
    scratch = [vmem(3, FIELDS, EDGE * 16, 128)]
    scratch += [vmem(size + 8, 128), vmem(size, 128)]
    scratch += [vmem(size + 8, 128), vmem(size + 8, 128), vmem(size, 128), vmem(size, 128)]
    scratch += [vmem(2, size + 112, 128)]
    scratch += [vmem(36, c * 8, 128) for c in (1, 3, 3, 4, 3)]
    for c in (1, 3, 3, 4, 3):
        scratch += [vmem(2, 2, c * 32, 128), vmem(2, 2, c * 8, 128)]
    scratch += [vmem(2, 34 * 32, 128), vmem(2, 34 * 24, 128)]
    scratch += [vmem(2, EDGE * 48, 128), vmem(2, EDGE * 24, 128), vmem(2, EDGE * 168, 128)]
    scratch += [vmem(2, size, 128)]
    dma = pltpu.SemaphoreType.DMA
    small = ((new_slot, pltpu.SMEM), (neighbor, pltpu.SMEM), (row_patch, pltpu.SMEM), (stress, pltpu.VMEM))
    scratch += [space(a.shape, a.dtype) for a, space in small]
    scratch += [dma((4,)), dma((CHUNKS,)), dma((2 * CHUNKS,)), dma((2 * CHUNKS,)), dma((10,)), dma((10,))]
    woven = state.reshape(2, 3, FIELDS, EDGE * 8, 128).transpose(1, 2, 3, 0, 4)
    outs = pl.pallas_call(
        make_kernel(columns, peers * columns),
        out_shape=tuple(pltpu.VMEM((n, EDGE * 16, 128), f32) for n in (FIELDS, 3)),
        in_specs=[pl.BlockSpec(memory_space=pltpu.HBM)] * 5,
        out_specs=(pl.BlockSpec(memory_space=pltpu.VMEM),) * 2,
        scratch_shapes=scratch,
        compiler_params=pltpu.CompilerParams(
            collective_id=0, has_side_effects=True, vmem_limit_bytes=36 * 2**20
        ),
    )(*(pltpu.with_memory_space_constraint(a, pltpu.HBM) for a in (woven.reshape(3, FIELDS, EDGE * 16, 128), new_slot, neighbor, stress, row_patch)))
    outs = pl.pallas_call(
        put_out,
        out_shape=tuple(jax.ShapeDtypeStruct((n, EDGE * 16, 128), f32) for n in (FIELDS, 3)),
        in_specs=[pl.BlockSpec(memory_space=pltpu.VMEM)] * 2,
        out_specs=(pl.BlockSpec(memory_space=pltpu.HBM),) * 2,
        scratch_shapes=[dma((2,))],
        compiler_params=pltpu.CompilerParams(vmem_limit_bytes=16 * 2**20),
    )(*outs)
    return tuple(
        out.reshape(-1, EDGE * 8, 2, 128).transpose(2, 0, 1, 3).reshape(2, -1, CELLS) for out in outs
    )


def solution(mesh):
    both = ("gz", "xy")
    in_specs = (P(both, None, None, None), P(both), P(both, None), P(both, None), P(both))
    out_specs = (P(both, None, None), P(both, None, None))
    return jax.shard_map(
        on_device, mesh=mesh, in_specs=in_specs, out_specs=out_specs, check_vma=False
    )
```

```python
import jax
import jax.numpy as jnp
from jax import lax
from jax.experimental import pallas as pl
from jax.experimental.pallas import tpu as pltpu
from jax.sharding import PartitionSpec as P

EDGE = 32
CELLS = EDGE**3
FIELDS = 7
OPPOSITE = (1, 0, 3, 2, 5, 4)
DIFFUSION = (0.8, 1.0, 0.6, 1.2, 0.9, 0.7)
GROWTH = (1.0, 0.5, 2.0, 1.5, 0.8, 1.2)
RATE = 6.0 / 11.0 * 0.02
MESH = pl.DeviceIdType.MESH


def iota(axis):
    return lax.broadcasted_iota(jnp.int32, (8, 128), axis)


def roll(v, shift, axis):
    if isinstance(shift, int) and shift % v.shape[axis] == 0:
        return v
    if isinstance(shift, int):
        shift = shift % v.shape[axis]
    return pltpu.roll(v, shift, axis)


def rows(start):
    return pl.ds(start if isinstance(start, int) else pl.multiple_of(start, 8), 8)


def pack(block, slot, fields, table, first, count):
    pitch = fields * 8
    lane = iota(1)
    own = (2 + slot) * 6
    table[own] = block[pl.ds(pitch + first * 8, count * 8), :]
    table[own + 1] = block[pl.ds(EDGE * pitch + first * 8, count * 8), :]
    for f in range(count):
        low = high = None
        for j in range(4):
            at = (8 * j + 1) * pitch + (first + f) * 8
            a = roll(block[pl.ds(at, 8, stride=pitch), :], 32 * j, 1)
            b = roll(block[pl.ds(at + 7, 8, stride=pitch), :], 32 * j + 32, 1)
            low = a if j == 0 else jnp.where(lane // 32 == j, a, low)
            high = b if j == 0 else jnp.where(lane // 32 == j, b, high)
        table[own + 2, pl.ds(f * 8, 8)] = low
        table[own + 3, pl.ds(f * 8, 8)] = high

    for f in range(count):
        low = high = None
        for x in range(EDGE):
            v = roll(block[pl.ds((x + 1) * pitch + (first + f) * 8, 8), :], x, 1)
            low = v if x == 0 else jnp.where(lane % 32 == x, v, low)
            high = v if x == 0 else jnp.where(lane % 32 == x - 1, v, high)
        table[own + 4, pl.ds(f * 8, 8)] = low
        table[own + 5, pl.ds(f * 8, 8)] = roll(high, 97, 1)


def fill(block, slot, fields, table, neighbor, lower, y_ghost, z_ghost, first, count):
    pitch = fields * 8
    for face in range(6):
        beyond = neighbor[slot, face]
        inside = beyond >= 0
        pick = jnp.where(inside, jnp.clip(beyond - lower, 0, 5), 2) * 6 + OPPOSITE[face]
        tile = jnp.where(inside, table[pick], 0.0)
        if face == 0:
            block[pl.ds(first * 8, count * 8), :] = tile
        elif face == 1:
            block[pl.ds((EDGE + 1) * pitch + first * 8, count * 8), :] = tile
        elif face < 4:
            for f in range(count):
                one = tile[f * 8 : f * 8 + 8]
                for j in range(4):
                    shift = -32 * j if face == 2 else 96 - 32 * j
                    y_ghost[face - 2, pl.ds(f * 32 + j * 8, 8)] = roll(one, shift, 1)
        else:
            z_ghost[face - 4] = tile


def nearby(block, fields, f, x, y_ghost, z_ghost, first=0):
    pitch = fields * 8
    lane, sub = iota(1), iota(0)
    at = (x + 1) * pitch + f * 8
    v = block[rows(at), :]
    f = f - first
    y_low = y_ghost[0, pl.ds(f * 32 + x, 1)]
    y_high = y_ghost[1, pl.ds(f * 32 + x, 1)]
    down = roll(v, 32, 1)
    up = roll(v, 96, 1)
    lower_y = jnp.where(lane < 32, jnp.where(sub == 0, y_low, roll(down, 1, 0)), down)
    upper_y = jnp.where(lane >= 96, jnp.where(sub == 7, y_high, roll(up, 7, 0)), up)
    z_low = roll(z_ghost[0, pl.ds(f * 8, 8)], 128 - x, 1)
    z_high = roll(z_ghost[1, pl.ds(f * 8, 8)], 31 - x + 128, 1)
    lower_z = jnp.where(lane % 32 == 0, z_low, roll(v, 1, 1))
    upper_z = jnp.where(lane % 32 == 31, z_high, roll(v, 127, 1))
    return v, (block[rows(at - pitch), :], block[rows(at + pitch), :], lower_y, upper_y, lower_z, upper_z)


def total(parts):
    return ((parts[0] + parts[1]) + (parts[2] + parts[3])) + (parts[4] + parts[5])


GROUPS = ((0, 1), (1, 3), (4, 3))


def make_kernel(columns, devices):
    def kernel(state, new_slot_in, neighbor_in, stress_in, row_patch_in, full_state, full_velocity, *scratch):
        scratch = iter(scratch)

        def take(count):
            return [next(scratch) for _ in range(count)]

        (levels,) = take(1)
        send_e, stay_e, came_e = take(3), take(3), take(3)
        send_h, stay_h, came_h = take(3)
        cells = take(3)
        first, second = take(4), take(3)
        tables, y_ghosts, z_ghosts = take(10), take(10), take(10)
        weight, force, slope, base = take(4)
        new_slot, neighbor, row_patch, stress = take(4)
        small_sem, load_sem, send_sem, recv_sem, face_send, face_recv = take(6)

        gz, xy = lax.axis_index("gz"), lax.axis_index("xy")
        device = gz * columns + xy
        left, right = device - 1, device + 1
        lower = (device - 1) * 2

        def place(d):
            return (d // columns, d % columns)

        loads = []
        for g, (low, count) in enumerate(GROUPS):
            part = pl.ds(low, count)
            loads.append(pltpu.make_async_copy(state.at[:, part], levels.at[:, part], load_sem.at[g]))
            loads[-1].start()

        small = []
        for k, (a, b) in enumerate(
            ((new_slot_in, new_slot), (neighbor_in, neighbor), (row_patch_in, row_patch), (stress_in, stress))
        ):
            small.append(pltpu.make_async_copy(a, b, small_sem.at[k]))
            small[-1].start()

        barrier = pltpu.get_barrier_semaphore()
        pl.semaphore_signal(barrier, inc=1, device_id=(1 - gz, xy), device_id_type=MESH)

        @pl.when(device > 0)
        def _():
            pl.semaphore_signal(barrier, inc=1, device_id=place(left), device_id_type=MESH)

        @pl.when(device < devices - 1)
        def _():
            pl.semaphore_signal(barrier, inc=1, device_id=place(right), device_id_type=MESH)

        @pl.when(device > 1)
        def _():
            pl.semaphore_signal(barrier, inc=1, device_id=place(device - 2), device_id_type=MESH)

        @pl.when(device < devices - 2)
        def _():
            pl.semaphore_signal(barrier, inc=1, device_id=place(device + 2), device_id_type=MESH)

        for copy in small:
            copy.wait()
        start = device * 2
        zero_stays = (new_slot[0] >= start) & (new_slot[0] < start + 2)
        stay_slot = jnp.where(zero_stays, new_slot[0], new_slot[1]) - start
        stays = [stay_slot == s for s in range(2)]

        sums = []
        for p in range(2):
            line = jnp.zeros((1, 128), jnp.float32)
            for r in range(stress.shape[0]):
                line = line + jnp.where(row_patch[r] == start + p, stress[r : r + 1, :], 0.0)
            sums.append(line)
        top = iota(0) == 0
        lines = pl.ds(EDGE * 8, 8)
        send_e[0][lines, :] = jnp.where(top, jnp.where(zero_stays, sums[1], sums[0]), 0.0)
        stay_e[0][lines, :] = jnp.where(top, jnp.where(zero_stays, sums[0], sums[1]), 0.0)

        def move(source, target, k):
            return pltpu.make_async_remote_copy(
                src_ref=source,
                dst_ref=target,
                send_sem=send_sem.at[k],
                recv_sem=recv_sem.at[k],
                device_id=(1 - gz, xy),
                device_id_type=MESH,
            )

        moves = [move(send_e[g], came_e[g], g) for g in range(3)] + [move(send_h, came_h, 3)]

        def combine_group(g):
            low, count = GROUPS[g]

            def combine(x, carry):
                for f in range(count):
                    to = rows((x * count + f) * 8)
                    to_h = rows((x * FIELDS + low + f) * 8)
                    both = []
                    for p in range(2):
                        part = pl.ds(x * 16 + p, 8, stride=2)
                        a, b, d = (levels.at[k, low + f][part, :] for k in range(3))
                        both.append(
                            (3.0 * a - 3.0 * b + d, (18.0 * a - 9.0 * b + 2.0 * d) * (1.0 / 11.0))
                        )
                    send_e[g][to, :] = jnp.where(zero_stays, both[1][0], both[0][0])
                    stay_e[g][to, :] = jnp.where(zero_stays, both[0][0], both[1][0])
                    send_h[to_h, :] = jnp.where(zero_stays, both[1][1], both[0][1])
                    stay_h[to_h, :] = jnp.where(zero_stays, both[0][1], both[1][1])
                return carry

            lax.fori_loop(0, EDGE, combine, 0, unroll=8 if count == 1 else 4)

        loads[0].wait()
        combine_group(0)
        below = (device + devices - 1) // devices + (device + devices - 2) // devices
        above = (2 * devices - 2 - device) // devices + (2 * devices - 3 - device) // devices
        pl.semaphore_wait(barrier, 1 + below + above)
        moves[0].start()
        for g in (1, 2):
            loads[g].wait()
            combine_group(g)
            moves[g].start()
        moves[3].start()

        def arrange_group(g):
            count = GROUPS[g][1]
            moves[g].wait_recv()

            def arrange(x, carry):
                part = pl.ds(pl.multiple_of(x * count * 8, 8), count * 8)
                to = pl.ds(pl.multiple_of((x + 1) * count * 8, 8), count * 8)
                here, there = stay_e[g][part, :], came_e[g][part, :]
                cells[g].at[0][to, :] = jnp.where(stays[0], here, there)
                cells[g].at[1][to, :] = jnp.where(stays[1], here, there)
                return carry

            lax.fori_loop(0, EDGE, arrange, 0, unroll=8 if count == 1 else 4)

        def faces(k, side):
            to, target = (0, right) if side == 0 else (24, left)
            return pltpu.make_async_remote_copy(
                src_ref=tables[k].at[pl.ds(12, 12)],
                dst_ref=tables[k].at[pl.ds(to, 12)],
                send_sem=face_send.at[2 * k + side],
                recv_sem=face_recv.at[2 * k + side],
                device_id=place(target),
                device_id_type=MESH,
            )

        def send_faces(k):
            @pl.when(device < devices - 1)
            def _():
                faces(k, 0).start()

            @pl.when(device > 0)
            def _():
                faces(k, 1).start()

        def await_faces(k):
            @pl.when(device > 0)
            def _():
                faces(k, 0).wait_recv()

            @pl.when(device < devices - 1)
            def _():
                faces(k, 1).wait_recv()

        odd = device % 2 == 1
        even = device % 2 == 0

        def hop(k, second_hop, source, to, target):
            return pltpu.make_async_remote_copy(
                src_ref=tables[k].at[pl.ds(source, 12)],
                dst_ref=tables[k].at[pl.ds(to, 12)],
                send_sem=face_send.at[2 * k + second_hop],
                recv_sem=face_recv.at[2 * k + second_hop],
                device_id=place(target),
                device_id_type=MESH,
            )

        def to_partner(k, act):
            @pl.when(even)
            def _():
                act(hop(k, 0, 12, 0, right))

            @pl.when(odd)
            def _():
                act(hop(k, 0, 12, 24, left))

        def to_second(k, act):
            @pl.when(even & (device < devices - 2))
            def _():
                act(hop(k, 1, 24, 0, device + 2))

            @pl.when(odd & (device > 1))
            def _():
                act(hop(k, 1, 0, 24, device - 2))

        def hand_on(k):
            @pl.when(even)
            def _():
                hop(k, 0, 12, 24, right).wait_recv()

            @pl.when(odd)
            def _():
                hop(k, 0, 12, 0, left).wait_recv()

            to_second(k, lambda copy: copy.start())

        def await_second(k):
            @pl.when(even & (device > 0))
            def _():
                hop(k, 1, 24, 0, device - 2).wait_recv()

            @pl.when(odd & (device < devices - 1))
            def _():
                hop(k, 1, 0, 24, device + 2).wait_recv()

        blocks = cells + first[:3] + [first[3]] + second
        widths = [1, 3, 3] + [1] * 7
        direct, relayed = (0, 3, 4, 5, 7, 8, 9), (1, 2, 6)

        def pack_table(k):
            for s in range(2):
                pack(blocks[k].at[s], s, widths[k], tables[k], 0, widths[k])

        def fill_table(k):
            for s in range(2):
                fill(
                    blocks[k].at[s], s, widths[k], tables[k], neighbor, lower,
                    y_ghosts[k].at[s], z_ghosts[k].at[s], 0, widths[k],
                )

        def around(k, s, f, x):
            return nearby(blocks[k].at[s], widths[k], f, x, y_ghosts[k].at[s], z_ghosts[k].at[s])

        def launch(k):
            if k in direct:
                send_faces(k)
            else:
                to_partner(k, lambda copy: copy.start())

        def begin(x, carry):
            for s in range(2):
                v, near = around(0, s, 0, x)
                viscous = jnp.exp(0.3 * v)
                sides = [(viscous + jnp.exp(0.3 * n)) * 0.5 for n in near]
                inverse = 1.0 / (viscous + total(sides))
                half = 0.25 * v
                for i in range(6):
                    weight.at[s][rows((x * 6 + i) * 8), :] = sides[i] * inverse
                for k in range(3):
                    f = half * (near[2 * k + 1] - near[2 * k])
                    if k == 0:
                        f = f + jnp.where(x == 0, traction[s], 0.0)
                    f = f * inverse
                    force.at[s][rows((x * 3 + k) * 8), :] = f
                    first[k].at[s][rows((x + 1) * 8), :] = f
                laplace = total(near) - 6.0 * v
                first[3].at[s][rows((x + 1) * 8), :] = v * v * v - v - 0.5 * laplace
            return carry

        def species(g):
            low, count = GROUPS[g]

            def step(x, carry):
                for s in range(2):
                    if g > 0:
                        phi = cells[0].at[s][rows((x + 1) * 8), :]
                        biofilm = 0.5 * (1.0 + jnp.tanh(phi))
                    for f in range(low, low + count):
                        at = rows((x * 7 + f) * 8)
                        v, near = around(g, s, f - low, x)
                        for k in range(3):
                            slope.at[s][rows(((x * 7 + f) * 3 + k) * 8), :] = (
                                near[2 * k + 1] - near[2 * k]
                            ) * (0.5 * RATE)
                        history = jnp.where(stays[s], stay_h[at, :], came_h[at, :])
                        if f > 0:
                            laplace = total(near) - 6.0 * v
                            uptake = GROWTH[f - 1] * biofilm * v / (0.5 + jnp.abs(v))
                            history = history + RATE * (DIFFUSION[f - 1] * laplace - uptake)
                        base.at[s][at, :] = history
                return carry

            lax.fori_loop(0, EDGE, step, 0, unroll=4 if count == 1 else 2)

        def coupled(k, c, s, x):
            near = around(k, s, 0, x)[1]
            sides = [weight.at[s][rows((x * 6 + i) * 8), :] for i in range(6)]
            return force.at[s][rows((x * 3 + c) * 8), :] + total([sides[i] * near[i] for i in range(6)])

        def sweep(c):
            def again(x, carry):
                for s in range(2):
                    second[c].at[s][rows((x + 1) * 8), :] = coupled(3 + c, c, s, x)
                return carry

            lax.fori_loop(0, EDGE, again, 0, unroll=8)

        def phase(x, carry):
            for s in range(2):
                v, near = around(6, s, 0, x)
                at = rows(x * 56)
                base.at[s][at, :] = base.at[s][at, :] + (0.2 * RATE) * (total(near) - 6.0 * v)
            return carry

        for g in range(3):
            arrange_group(g)
            pack_table(g)
            launch(g)
        traction = [jnp.where(stays[s], stay_e[0][lines, :], came_e[0][lines, :]) for s in range(2)]

        await_faces(0)
        fill_table(0)
        lax.fori_loop(0, EDGE, begin, 0, unroll=4)
        for k in (3, 4, 5, 6):
            pack_table(k)
            launch(k)
        hand_on(1)
        moves[3].wait_recv()
        species(0)
        hand_on(2)
        for c in range(3):
            await_faces(3 + c)
            fill_table(3 + c)
            sweep(c)
            pack_table(7 + c)
            launch(7 + c)
        hand_on(6)
        for g in (1, 2):
            await_second(g)
            fill_table(g)
            species(g)
        await_second(6)
        fill_table(6)
        lax.fori_loop(0, EDGE, phase, 0, unroll=4)
        for c in range(3):
            await_faces(7 + c)
            fill_table(7 + c)

        def finish(x, carry):
            for s in range(2):
                velocity = [coupled(7 + c, c, s, x) for c in range(3)]
                to = pl.ds(x * 16 + s, 8, stride=2)
                for k in range(3):
                    full_velocity.at[k][to, :] = velocity[k]
                for f in range(FIELDS):
                    advect = [
                        velocity[k] * slope.at[s][rows(((x * 7 + f) * 3 + k) * 8), :] for k in range(3)
                    ]
                    kept = base.at[s][rows((x * 7 + f) * 8), :]
                    full_state.at[f][to, :] = kept - (advect[0] + advect[1] + advect[2])
            return carry

        lax.fori_loop(0, EDGE, finish, 0, unroll=4)

        for copy in moves:
            copy.wait_send()
        for k in direct:

            @pl.when(device < devices - 1)
            def _():
                faces(k, 0).wait_send()

            @pl.when(device > 0)
            def _():
                faces(k, 1).wait_send()

        for k in relayed:
            to_partner(k, lambda copy: copy.wait_send())
            to_second(k, lambda copy: copy.wait_send())

    return kernel


def put_out(state, velocity, out_state, out_velocity, sem):
    copies = [
        pltpu.make_async_copy(state, out_state, sem.at[0]),
        pltpu.make_async_copy(velocity, out_velocity, sem.at[1]),
    ]
    for copy in copies:
        copy.start()
    for copy in copies:
        copy.wait()


def on_device(state, new_slot, neighbor, stress, row_patch):
    peers, columns = lax.axis_size("gz"), lax.axis_size("xy")
    assert peers == 2 and state.shape == (2, 3, FIELDS, CELLS)
    f32 = jnp.float32

    def vmem(*shape):
        return pltpu.VMEM(shape, f32)

    scratch = [vmem(3, FIELDS, EDGE * 16, 128)]
    for _ in range(3):
        scratch += [vmem(EDGE * 8 + 8, 128), vmem(EDGE * 24, 128), vmem(EDGE * 24, 128)]
    scratch += [vmem(EDGE * 56, 128)] * 3
    widths = (1, 3, 3) + (1,) * 7
    scratch += [vmem(2, 34 * c * 8, 128) for c in widths]
    scratch += [vmem(36, c * 8, 128) for c in widths]
    scratch += [vmem(2, 2, c * 32, 128) for c in widths]
    scratch += [vmem(2, 2, c * 8, 128) for c in widths]
    scratch += [vmem(2, EDGE * 48, 128), vmem(2, EDGE * 24, 128), vmem(2, EDGE * 168, 128)]
    scratch += [vmem(2, EDGE * 56, 128)]
    dma = pltpu.SemaphoreType.DMA
    small = ((new_slot, pltpu.SMEM), (neighbor, pltpu.SMEM), (row_patch, pltpu.SMEM), (stress, pltpu.VMEM))
    scratch += [space(a.shape, a.dtype) for a, space in small]
    scratch += [dma((n,)) for n in (4, 3, 4, 4, 20, 20)]
    woven = state.reshape(2, 3, FIELDS, EDGE * 8, 128).transpose(1, 2, 3, 0, 4)
    outs = pl.pallas_call(
        make_kernel(columns, peers * columns),
        out_shape=tuple(pltpu.VMEM((n, EDGE * 16, 128), f32) for n in (FIELDS, 3)),
        in_specs=[pl.BlockSpec(memory_space=pltpu.HBM)] * 5,
        out_specs=(pl.BlockSpec(memory_space=pltpu.VMEM),) * 2,
        scratch_shapes=scratch,
        compiler_params=pltpu.CompilerParams(
            collective_id=0, has_side_effects=True, vmem_limit_bytes=36 * 2**20
        ),
    )(*(pltpu.with_memory_space_constraint(a, pltpu.HBM) for a in (woven.reshape(3, FIELDS, EDGE * 16, 128), new_slot, neighbor, stress, row_patch)))
    outs = pl.pallas_call(
        put_out,
        out_shape=tuple(jax.ShapeDtypeStruct((n, EDGE * 16, 128), f32) for n in (FIELDS, 3)),
        in_specs=[pl.BlockSpec(memory_space=pltpu.VMEM)] * 2,
        out_specs=(pl.BlockSpec(memory_space=pltpu.HBM),) * 2,
        scratch_shapes=[dma((2,))],
        compiler_params=pltpu.CompilerParams(vmem_limit_bytes=16 * 2**20),
    )(*outs)
    return tuple(
        out.reshape(-1, EDGE * 8, 2, 128).transpose(2, 0, 1, 3).reshape(2, -1, CELLS) for out in outs
    )


def solution(mesh):
    both = ("gz", "xy")
    in_specs = (P(both, None, None, None), P(both), P(both, None), P(both, None), P(both))
    out_specs = (P(both, None, None), P(both, None, None))
    return jax.shard_map(
        on_device, mesh=mesh, in_specs=in_specs, out_specs=out_specs, check_vma=False
    )
```

```python
import jax
import jax.numpy as jnp
from jax import lax
from jax.experimental import pallas as pl
from jax.experimental.pallas import tpu as pltpu
from jax.sharding import PartitionSpec as P

EDGE = 32
CELLS = EDGE**3
FIELDS = 7
OPPOSITE = (1, 0, 3, 2, 5, 4)
DIFFUSION = (0.8, 1.0, 0.6, 1.2, 0.9, 0.7)
GROWTH = (1.0, 0.5, 2.0, 1.5, 0.8, 1.2)
RATE = 6.0 / 11.0 * 0.02
MESH = pl.DeviceIdType.MESH


def iota(axis):
    return lax.broadcasted_iota(jnp.int32, (8, 128), axis)


def roll(v, shift, axis):
    if isinstance(shift, int) and shift % v.shape[axis] == 0:
        return v
    if isinstance(shift, int):
        shift = shift % v.shape[axis]
    return pltpu.roll(v, shift, axis)


def rows(start):
    return pl.ds(start if isinstance(start, int) else pl.multiple_of(start, 8), 8)


def pack(block, slot, fields, table, first, count):
    pitch = fields * 8
    lane = iota(1)
    own = (2 + slot) * 6
    table[own] = block[pl.ds(pitch + first * 8, count * 8), :]
    table[own + 1] = block[pl.ds(EDGE * pitch + first * 8, count * 8), :]
    for f in range(count):
        low = high = None
        for j in range(4):
            at = (8 * j + 1) * pitch + (first + f) * 8
            a = roll(block[pl.ds(at, 8, stride=pitch), :], 32 * j, 1)
            b = roll(block[pl.ds(at + 7, 8, stride=pitch), :], 32 * j + 32, 1)
            low = a if j == 0 else jnp.where(lane // 32 == j, a, low)
            high = b if j == 0 else jnp.where(lane // 32 == j, b, high)
        table[own + 2, pl.ds(f * 8, 8)] = low
        table[own + 3, pl.ds(f * 8, 8)] = high

    for f in range(count):
        low = high = None
        for x in range(EDGE):
            v = roll(block[pl.ds((x + 1) * pitch + (first + f) * 8, 8), :], x, 1)
            low = v if x == 0 else jnp.where(lane % 32 == x, v, low)
            high = v if x == 0 else jnp.where(lane % 32 == x - 1, v, high)
        table[own + 4, pl.ds(f * 8, 8)] = low
        table[own + 5, pl.ds(f * 8, 8)] = roll(high, 97, 1)


def fill(block, slot, fields, table, neighbor, lower, y_ghost, z_ghost, first, count):
    pitch = fields * 8
    for face in range(6):
        beyond = neighbor[slot, face]
        inside = beyond >= 0
        pick = jnp.where(inside, jnp.clip(beyond - lower, 0, 5), 2) * 6 + OPPOSITE[face]
        tile = jnp.where(inside, table[pick], 0.0)
        if face == 0:
            block[pl.ds(first * 8, count * 8), :] = tile
        elif face == 1:
            block[pl.ds((EDGE + 1) * pitch + first * 8, count * 8), :] = tile
        elif face < 4:
            for f in range(count):
                one = tile[f * 8 : f * 8 + 8]
                for j in range(4):
                    shift = -32 * j if face == 2 else 96 - 32 * j
                    y_ghost[face - 2, pl.ds(f * 32 + j * 8, 8)] = roll(one, shift, 1)
        else:
            z_ghost[face - 4] = tile


def nearby(block, fields, f, x, y_ghost, z_ghost, first=0):
    pitch = fields * 8
    lane, sub = iota(1), iota(0)
    at = (x + 1) * pitch + f * 8
    v = block[rows(at), :]
    f = f - first
    y_low = y_ghost[0, pl.ds(f * 32 + x, 1)]
    y_high = y_ghost[1, pl.ds(f * 32 + x, 1)]
    down = roll(v, 32, 1)
    up = roll(v, 96, 1)
    lower_y = jnp.where(lane < 32, jnp.where(sub == 0, y_low, roll(down, 1, 0)), down)
    upper_y = jnp.where(lane >= 96, jnp.where(sub == 7, y_high, roll(up, 7, 0)), up)
    z_low = roll(z_ghost[0, pl.ds(f * 8, 8)], 128 - x, 1)
    z_high = roll(z_ghost[1, pl.ds(f * 8, 8)], 31 - x + 128, 1)
    lower_z = jnp.where(lane % 32 == 0, z_low, roll(v, 1, 1))
    upper_z = jnp.where(lane % 32 == 31, z_high, roll(v, 127, 1))
    return v, (block[rows(at - pitch), :], block[rows(at + pitch), :], lower_y, upper_y, lower_z, upper_z)


def inside(block, fields, f, x):
    pitch = fields * 8
    lane, sub = iota(1), iota(0)
    at = (x + 1) * pitch + f * 8
    v = block[rows(at), :]
    down = roll(v, 32, 1)
    up = roll(v, 96, 1)
    lower_y = jnp.where(lane < 32, jnp.where(sub == 0, 0.0, roll(down, 1, 0)), down)
    upper_y = jnp.where(lane >= 96, jnp.where(sub == 7, 0.0, roll(up, 7, 0)), up)
    lower_z = jnp.where(lane % 32 == 0, 0.0, roll(v, 1, 1))
    upper_z = jnp.where(lane % 32 == 31, 0.0, roll(v, 127, 1))
    return v, (block[rows(at - pitch), :], block[rows(at + pitch), :], lower_y, upper_y, lower_z, upper_z)


def total(parts):
    return ((parts[0] + parts[1]) + (parts[2] + parts[3])) + (parts[4] + parts[5])


GROUPS = ((0, 1), (1, 3), (4, 3))
DIRECT = (0, 7, 8, 9)
MIXED = ()
PLAN = (
    ("arrange", 0),
    ("send", 0),
    ("arrange", 1),
    ("send", 1),
    ("arrange", 2),
    ("history", 0),
    ("interior", 1),
    ("collect", 0),
    ("begin", 0),
    ("send", 3),
    ("send", 4),
    ("send", 5),
    ("relay", 1),
    ("send", 2),
    ("send", 6),
    ("species", 0),
    ("relay", 3),
    ("relay", 4),
    ("relay", 5),
    ("interior", 2),
    ("collect", 3),
    ("sweep", 0),
    ("send", 7),
    ("relay", 2),
    ("collect", 4),
    ("sweep", 1),
    ("send", 8),
    ("collect", 5),
    ("sweep", 2),
    ("send", 9),
    ("relay", 6),
    ("collect", 1),
    ("border", 1),
    ("collect", 2),
    ("border", 2),
    ("collect", 6),
    ("phase", 0),
    ("collect", 7),
    ("collect", 8),
    ("collect", 9),
    ("finish", 0),
)


def make_kernel(columns, devices):
    def kernel(state, new_slot_in, neighbor_in, stress_in, row_patch_in, full_state, full_velocity, *scratch):
        scratch = iter(scratch)

        def take(count):
            return [next(scratch) for _ in range(count)]

        (levels,) = take(1)
        send_e, stay_e, came_e = take(3), take(3), take(3)
        send_h, stay_h, came_h = take(3)
        cells = take(3)
        first, second = take(4), take(3)
        tables, y_ghosts, z_ghosts = take(10), take(10), take(10)
        weight, force, slope, base = take(4)
        new_slot, neighbor, row_patch, stress = take(4)
        small_sem, load_sem, send_sem, recv_sem, face_send, face_recv = take(6)

        gz, xy = lax.axis_index("gz"), lax.axis_index("xy")
        device = gz * columns + xy
        left, right = device - 1, device + 1
        lower = (device - 1) * 2

        def place(d):
            return (d // columns, d % columns)

        loads = []
        for g, (low, count) in enumerate(GROUPS):
            part = pl.ds(low, count)
            loads.append(pltpu.make_async_copy(state.at[:, part], levels.at[:, part], load_sem.at[g]))
            loads[-1].start()

        small = []
        for k, (a, b) in enumerate(
            ((new_slot_in, new_slot), (neighbor_in, neighbor), (row_patch_in, row_patch), (stress_in, stress))
        ):
            small.append(pltpu.make_async_copy(a, b, small_sem.at[k]))
            small[-1].start()

        barrier = pltpu.get_barrier_semaphore()
        pl.semaphore_signal(barrier, inc=1, device_id=(1 - gz, xy), device_id_type=MESH)

        @pl.when(device > 0)
        def _():
            pl.semaphore_signal(barrier, inc=1, device_id=place(left), device_id_type=MESH)

        @pl.when(device < devices - 1)
        def _():
            pl.semaphore_signal(barrier, inc=1, device_id=place(right), device_id_type=MESH)

        @pl.when(device > 1)
        def _():
            pl.semaphore_signal(barrier, inc=1, device_id=place(device - 2), device_id_type=MESH)

        @pl.when(device < devices - 2)
        def _():
            pl.semaphore_signal(barrier, inc=1, device_id=place(device + 2), device_id_type=MESH)

        for copy in small:
            copy.wait()
        own = device * 2
        zero_stays = (new_slot[0] >= own) & (new_slot[0] < own + 2)
        stay_slot = jnp.where(zero_stays, new_slot[0], new_slot[1]) - own
        stays = [stay_slot == s for s in range(2)]

        sums = []
        for p in range(2):
            line = jnp.zeros((1, 128), jnp.float32)
            for r in range(stress.shape[0]):
                line = line + jnp.where(row_patch[r] == own + p, stress[r : r + 1, :], 0.0)
            sums.append(line)
        top = iota(0) == 0
        lines = pl.ds(EDGE * 8, 8)
        send_e[0][lines, :] = jnp.where(top, jnp.where(zero_stays, sums[1], sums[0]), 0.0)
        stay_e[0][lines, :] = jnp.where(top, jnp.where(zero_stays, sums[0], sums[1]), 0.0)

        def move(source, target, k):
            return pltpu.make_async_remote_copy(
                src_ref=source,
                dst_ref=target,
                send_sem=send_sem.at[k],
                recv_sem=recv_sem.at[k],
                device_id=(1 - gz, xy),
                device_id_type=MESH,
            )

        moves = [move(send_e[g], came_e[g], g) for g in range(3)] + [move(send_h, came_h, 3)]

        def combine_group(g):
            low, count = GROUPS[g]

            def combine(x, carry):
                for f in range(count):
                    to = rows((x * count + f) * 8)
                    to_h = rows((x * FIELDS + low + f) * 8)
                    both = []
                    for p in range(2):
                        part = pl.ds(x * 16 + p, 8, stride=2)
                        a, b, d = (levels.at[k, low + f][part, :] for k in range(3))
                        both.append(
                            (3.0 * a - 3.0 * b + d, (18.0 * a - 9.0 * b + 2.0 * d) * (1.0 / 11.0))
                        )
                    send_e[g][to, :] = jnp.where(zero_stays, both[1][0], both[0][0])
                    stay_e[g][to, :] = jnp.where(zero_stays, both[0][0], both[1][0])
                    send_h[to_h, :] = jnp.where(zero_stays, both[1][1], both[0][1])
                    stay_h[to_h, :] = jnp.where(zero_stays, both[0][1], both[1][1])
                return carry

            lax.fori_loop(0, EDGE, combine, 0, unroll=8 if count == 1 else 4)

        loads[0].wait()
        combine_group(0)
        below = (device + devices - 1) // devices + (device + devices - 2) // devices
        above = (2 * devices - 2 - device) // devices + (2 * devices - 3 - device) // devices
        pl.semaphore_wait(barrier, 1 + below + above)
        moves[0].start()
        for g in (1, 2):
            loads[g].wait()
            combine_group(g)
            moves[g].start()
        moves[3].start()

        def arrange_group(g):
            count = GROUPS[g][1]
            moves[g].wait_recv()

            def arrange(x, carry):
                part = pl.ds(pl.multiple_of(x * count * 8, 8), count * 8)
                to = pl.ds(pl.multiple_of((x + 1) * count * 8, 8), count * 8)
                here, there = stay_e[g][part, :], came_e[g][part, :]
                cells[g].at[0][to, :] = jnp.where(stays[0], here, there)
                cells[g].at[1][to, :] = jnp.where(stays[1], here, there)
                return carry

            lax.fori_loop(0, EDGE, arrange, 0, unroll=8 if count == 1 else 4)

        half = devices // 2
        odd = device % 2 == 1
        even = device % 2 == 0

        def send_to(k, which, source, to, target):
            return pltpu.make_async_remote_copy(
                src_ref=tables[k].at[pl.ds(source, 12)],
                dst_ref=tables[k].at[pl.ds(to, 12)],
                send_sem=face_send.at[3 * k + which],
                recv_sem=face_recv.at[3 * k + which],
                device_id=place(target),
                device_id_type=MESH,
            )

        def at(condition, act, *copy):
            @pl.when(condition)
            def _():
                act(send_to(*copy))

        def start(copy):
            copy.start()

        def arrive(copy):
            copy.wait_recv()

        def leave(copy):
            copy.wait_send()

        splits = [devices if k in DIRECT else half if k in MIXED else 0 for k in range(10)]

        def outward(k, act):
            split = splits[k]
            if split > 0:
                at(device < split - 1, act, k, 0, 12, 0, right)
                at((device > 0) & (device < split), act, k, 1, 12, 24, left)
            if 0 < split < devices:
                at(device == split - 1, act, k, 2, 12, 0, right)
                at(device == split, act, k, 2, 12, 24, left)
            if split < devices:
                at((device >= split) & even, act, k, 0, 12, 0, right)
                at((device >= split) & odd, act, k, 0, 12, 24, left)

        def onward(k, act):
            split = splits[k]
            if split < devices:
                at(even & (device >= split) & (device < devices - 2), act, k, 1, 24, 0, device + 2)
                at(odd & (device >= split + 2), act, k, 1, 0, 24, device - 2)

        def launch(k):
            outward(k, start)

        def hand_on(k):
            split = splits[k]
            if split < devices:
                at((device >= split) & even, arrive, k, 0, 12, 24, right)
                at((device >= split) & odd, arrive, k, 0, 12, 0, left)
                onward(k, start)

        def collect(k):
            split = splits[k]
            if split > 0:
                at((device < split) & (device > 0), arrive, k, 0, 12, 0, right)
                at(device < split - 1, arrive, k, 1, 12, 24, left)
            if 0 < split < devices:
                at(device == split - 1, arrive, k, 2, 12, 24, right)
                at(device == split, arrive, k, 2, 12, 0, left)
            if split < devices:
                at(even & (device > split), arrive, k, 1, 24, 0, left)
                at(odd & (device >= split) & (device < devices - 1), arrive, k, 1, 0, 24, right)
            fill_table(k)

        blocks = cells + first[:3] + [first[3]] + second
        widths = [1, 3, 3] + [1] * 7

        def pack_table(k):
            for s in range(2):
                pack(blocks[k].at[s], s, widths[k], tables[k], 0, widths[k])

        def fill_table(k):
            for s in range(2):
                fill(
                    blocks[k].at[s], s, widths[k], tables[k], neighbor, lower,
                    y_ghosts[k].at[s], z_ghosts[k].at[s], 0, widths[k],
                )

        def around(k, s, f, x):
            return nearby(blocks[k].at[s], widths[k], f, x, y_ghosts[k].at[s], z_ghosts[k].at[s])

        def begin(x, carry, traction):
            for s in range(2):
                v, near = around(0, s, 0, x)
                viscous = jnp.exp(0.3 * v)
                sides = [(viscous + jnp.exp(0.3 * n)) * 0.5 for n in near]
                inverse = 1.0 / (viscous + total(sides))
                half = 0.25 * v
                for i in range(6):
                    weight.at[s][rows((x * 6 + i) * 8), :] = sides[i] * inverse
                for k in range(3):
                    f = half * (near[2 * k + 1] - near[2 * k])
                    if k == 0:
                        f = f + jnp.where(x == 0, traction[s], 0.0)
                    f = f * inverse
                    force.at[s][rows((x * 3 + k) * 8), :] = f
                    first[k].at[s][rows((x + 1) * 8), :] = f
                laplace = total(near) - 6.0 * v
                first[3].at[s][rows((x + 1) * 8), :] = v * v * v - v - 0.5 * laplace
            return carry

        def species_step(g, within):
            low, count = GROUPS[g]

            def step(x, carry):
                for s in range(2):
                    if g > 0:
                        phi = cells[0].at[s][rows((x + 1) * 8), :]
                        biofilm = 0.5 * (1.0 + jnp.tanh(phi))
                    for f in range(low, low + count):
                        to = rows((x * 7 + f) * 8)
                        if within:
                            v, near = inside(cells[g].at[s], count, f - low, x)
                        else:
                            v, near = around(g, s, f - low, x)
                        for k in range(3):
                            slope.at[s][rows(((x * 7 + f) * 3 + k) * 8), :] = (
                                near[2 * k + 1] - near[2 * k]
                            ) * (0.5 * RATE)
                        history = jnp.where(stays[s], stay_h[to, :], came_h[to, :])
                        if f > 0:
                            laplace = total(near) - 6.0 * v
                            uptake = GROWTH[f - 1] * biofilm * v / (0.5 + jnp.abs(v))
                            history = history + RATE * (DIFFUSION[f - 1] * laplace - uptake)
                        base.at[s][to, :] = history
                return carry

            return step

        def species(g):
            lax.fori_loop(0, EDGE, species_step(g, False), 0, unroll=4)

        def interior(g):
            lax.fori_loop(1, EDGE - 1, species_step(g, True), 0, unroll=3)

        def border(g):
            low, count = GROUPS[g]
            full = species_step(g, False)
            full(0, 0)
            full(EDGE - 1, 0)
            lane, sub = iota(1), iota(0)
            y_first = (lane < 32) & (sub == 0)
            y_last = (lane >= 96) & (sub == 7)
            z_first, z_last = lane % 32 == 0, lane % 32 == 31

            def weights(first_mask, last_mask):
                c = 0.5 * RATE
                sign = jnp.where(first_mask, -c, jnp.where(last_mask, c, 0.0))
                return sign, jnp.where(first_mask | last_mask, RATE, 0.0)

            y_sign, y_weight = weights(y_first, y_last)
            z_sign, z_weight = weights(z_first, z_last)

            def fix(x, carry):
                for s in range(2):
                    yg, zg = y_ghosts[g].at[s], z_ghosts[g].at[s]
                    for f in range(count):
                        y = jnp.where(y_first, yg[0, pl.ds(f * 32 + x, 1)], yg[1, pl.ds(f * 32 + x, 1)])
                        z_low = roll(zg[0, pl.ds(f * 8, 8)], 128 - x, 1)
                        z_high = roll(zg[1, pl.ds(f * 8, 8)], 31 - x + 128, 1)
                        z = jnp.where(z_first, z_low, z_high)
                        to = (x * 7 + low + f) * 8
                        for k, part in ((1, y * y_sign), (2, z * z_sign)):
                            here = rows(to * 3 + k * 8)
                            slope.at[s][here, :] = slope.at[s][here, :] + part
                        here = rows(to)
                        part = DIFFUSION[low + f - 1] * (y * y_weight + z * z_weight)
                        base.at[s][here, :] = base.at[s][here, :] + part
                return carry

            lax.fori_loop(1, EDGE - 1, fix, 0, unroll=3)

        def coupled(k, c, s, x):
            near = around(k, s, 0, x)[1]
            sides = [weight.at[s][rows((x * 6 + i) * 8), :] for i in range(6)]
            return force.at[s][rows((x * 3 + c) * 8), :] + total([sides[i] * near[i] for i in range(6)])

        def sweep(c):
            def again(x, carry):
                for s in range(2):
                    second[c].at[s][rows((x + 1) * 8), :] = coupled(3 + c, c, s, x)
                return carry

            lax.fori_loop(0, EDGE, again, 0, unroll=8)

        def phase(x, carry):
            for s in range(2):
                v, near = around(6, s, 0, x)
                at = rows(x * 56)
                base.at[s][at, :] = base.at[s][at, :] + (0.2 * RATE) * (total(near) - 6.0 * v)
            return carry

        def finish(x, carry):
            for s in range(2):
                velocity = [coupled(7 + c, c, s, x) for c in range(3)]
                to = pl.ds(x * 16 + s, 8, stride=2)
                for k in range(3):
                    full_velocity.at[k][to, :] = velocity[k]
                for f in range(FIELDS):
                    advect = [
                        velocity[k] * slope.at[s][rows(((x * 7 + f) * 3 + k) * 8), :] for k in range(3)
                    ]
                    kept = base.at[s][rows((x * 7 + f) * 8), :]
                    full_state.at[f][to, :] = kept - (advect[0] + advect[1] + advect[2])
            return carry

        def flow():
            traction = [jnp.where(stays[s], stay_e[0][lines, :], came_e[0][lines, :]) for s in range(2)]
            lax.fori_loop(0, EDGE, lambda x, carry: begin(x, carry, traction), 0, unroll=4)

        acts = {
            "arrange": arrange_group,
            "pack": pack_table,
            "send": launch,
            "relay": hand_on,
            "collect": collect,
            "begin": lambda _: flow(),
            "sweep": sweep,
            "history": lambda _: moves[3].wait_recv(),
            "species": species,
            "interior": interior,
            "border": border,
            "phase": lambda _: lax.fori_loop(0, EDGE, phase, 0, unroll=4),
            "finish": lambda _: lax.fori_loop(0, EDGE, finish, 0, unroll=4),
        }
        for act, which in PLAN:
            if act == "send":
                pack_table(which)
            acts[act](which)

        for copy in moves:
            copy.wait_send()
        for k in range(10):
            outward(k, leave)
            onward(k, leave)

    return kernel


def put_out(state, velocity, out_state, out_velocity, sem):
    copies = [
        pltpu.make_async_copy(state, out_state, sem.at[0]),
        pltpu.make_async_copy(velocity, out_velocity, sem.at[1]),
    ]
    for copy in copies:
        copy.start()
    for copy in copies:
        copy.wait()


def on_device(state, new_slot, neighbor, stress, row_patch):
    peers, columns = lax.axis_size("gz"), lax.axis_size("xy")
    assert peers == 2 and state.shape == (2, 3, FIELDS, CELLS)
    f32 = jnp.float32

    def vmem(*shape):
        return pltpu.VMEM(shape, f32)

    scratch = [vmem(3, FIELDS, EDGE * 16, 128)]
    for _ in range(3):
        scratch += [vmem(EDGE * 8 + 8, 128), vmem(EDGE * 24, 128), vmem(EDGE * 24, 128)]
    scratch += [vmem(EDGE * 56, 128)] * 3
    widths = (1, 3, 3) + (1,) * 7
    scratch += [vmem(2, 34 * c * 8, 128) for c in widths]
    scratch += [vmem(36, c * 8, 128) for c in widths]
    scratch += [vmem(2, 2, c * 32, 128) for c in widths]
    scratch += [vmem(2, 2, c * 8, 128) for c in widths]
    scratch += [vmem(2, EDGE * 48, 128), vmem(2, EDGE * 24, 128), vmem(2, EDGE * 168, 128)]
    scratch += [vmem(2, EDGE * 56, 128)]
    dma = pltpu.SemaphoreType.DMA
    small = ((new_slot, pltpu.SMEM), (neighbor, pltpu.SMEM), (row_patch, pltpu.SMEM), (stress, pltpu.VMEM))
    scratch += [space(a.shape, a.dtype) for a, space in small]
    scratch += [dma((n,)) for n in (4, 3, 4, 4, 30, 30)]
    woven = state.reshape(2, 3, FIELDS, EDGE * 8, 128).transpose(1, 2, 3, 0, 4)
    outs = pl.pallas_call(
        make_kernel(columns, peers * columns),
        out_shape=tuple(pltpu.VMEM((n, EDGE * 16, 128), f32) for n in (FIELDS, 3)),
        in_specs=[pl.BlockSpec(memory_space=pltpu.HBM)] * 5,
        out_specs=(pl.BlockSpec(memory_space=pltpu.VMEM),) * 2,
        scratch_shapes=scratch,
        compiler_params=pltpu.CompilerParams(
            collective_id=0, has_side_effects=True, vmem_limit_bytes=36 * 2**20
        ),
    )(*(pltpu.with_memory_space_constraint(a, pltpu.HBM) for a in (woven.reshape(3, FIELDS, EDGE * 16, 128), new_slot, neighbor, stress, row_patch)))
    outs = pl.pallas_call(
        put_out,
        out_shape=tuple(jax.ShapeDtypeStruct((n, EDGE * 16, 128), f32) for n in (FIELDS, 3)),
        in_specs=[pl.BlockSpec(memory_space=pltpu.VMEM)] * 2,
        out_specs=(pl.BlockSpec(memory_space=pltpu.HBM),) * 2,
        scratch_shapes=[dma((2,))],
        compiler_params=pltpu.CompilerParams(vmem_limit_bytes=16 * 2**20),
    )(*outs)
    return tuple(
        out.reshape(-1, EDGE * 8, 2, 128).transpose(2, 0, 1, 3).reshape(2, -1, CELLS) for out in outs
    )


def solution(mesh):
    both = ("gz", "xy")
    in_specs = (P(both, None, None, None), P(both), P(both, None), P(both, None), P(both))
    out_specs = (P(both, None, None), P(both, None, None))
    return jax.shard_map(
        on_device, mesh=mesh, in_specs=in_specs, out_specs=out_specs, check_vma=False
    )
```

```python
import jax
import jax.numpy as jnp
from jax import lax
from jax.experimental import pallas as pl
from jax.experimental.pallas import tpu as pltpu
from jax.sharding import PartitionSpec as P

EDGE = 32
CELLS = EDGE**3
FIELDS = 7
OPPOSITE = (1, 0, 3, 2, 5, 4)
DIFFUSION = (0.8, 1.0, 0.6, 1.2, 0.9, 0.7)
GROWTH = (1.0, 0.5, 2.0, 1.5, 0.8, 1.2)
RATE = 6.0 / 11.0 * 0.02
MESH = pl.DeviceIdType.MESH


def iota(axis):
    return lax.broadcasted_iota(jnp.int32, (8, 128), axis)


def roll(v, shift, axis):
    if isinstance(shift, int) and shift % v.shape[axis] == 0:
        return v
    if isinstance(shift, int):
        shift = shift % v.shape[axis]
    return pltpu.roll(v, shift, axis)


def rows(start):
    return pl.ds(start if isinstance(start, int) else pl.multiple_of(start, 8), 8)


def pack(block, slot, fields, table, first, count):
    pitch = fields * 8
    lane = iota(1)
    own = (2 + slot) * 6
    table[own] = block[pl.ds(pitch + first * 8, count * 8), :]
    table[own + 1] = block[pl.ds(EDGE * pitch + first * 8, count * 8), :]
    for f in range(count):
        low = high = None
        for j in range(4):
            at = (8 * j + 1) * pitch + (first + f) * 8
            a = roll(block[pl.ds(at, 8, stride=pitch), :], 32 * j, 1)
            b = roll(block[pl.ds(at + 7, 8, stride=pitch), :], 32 * j + 32, 1)
            low = a if j == 0 else jnp.where(lane // 32 == j, a, low)
            high = b if j == 0 else jnp.where(lane // 32 == j, b, high)
        table[own + 2, pl.ds(f * 8, 8)] = low
        table[own + 3, pl.ds(f * 8, 8)] = high

    for f in range(count):
        low = high = None
        for x in range(EDGE):
            v = roll(block[pl.ds((x + 1) * pitch + (first + f) * 8, 8), :], x, 1)
            low = v if x == 0 else jnp.where(lane % 32 == x, v, low)
            high = v if x == 0 else jnp.where(lane % 32 == x - 1, v, high)
        table[own + 4, pl.ds(f * 8, 8)] = low
        table[own + 5, pl.ds(f * 8, 8)] = roll(high, 97, 1)


def fill(block, slot, fields, table, neighbor, lower, y_ghost, z_ghost, first, count):
    pitch = fields * 8
    for face in range(6):
        beyond = neighbor[slot, face]
        inside = beyond >= 0
        pick = jnp.where(inside, jnp.clip(beyond - lower, 0, 5), 2) * 6 + OPPOSITE[face]
        tile = jnp.where(inside, table[pick], 0.0)
        if face == 0:
            block[pl.ds(first * 8, count * 8), :] = tile
        elif face == 1:
            block[pl.ds((EDGE + 1) * pitch + first * 8, count * 8), :] = tile
        elif face < 4:
            for f in range(count):
                one = tile[f * 8 : f * 8 + 8]
                for j in range(4):
                    shift = -32 * j if face == 2 else 96 - 32 * j
                    y_ghost[face - 2, pl.ds(f * 32 + j * 8, 8)] = roll(one, shift, 1)
        else:
            z_ghost[face - 4] = tile


def nearby(block, fields, f, x, y_ghost, z_ghost, first=0):
    pitch = fields * 8
    lane, sub = iota(1), iota(0)
    at = (x + 1) * pitch + f * 8
    v = block[rows(at), :]
    f = f - first
    y_low = y_ghost[0, pl.ds(f * 32 + x, 1)]
    y_high = y_ghost[1, pl.ds(f * 32 + x, 1)]
    down = roll(v, 32, 1)
    up = roll(v, 96, 1)
    lower_y = jnp.where(lane < 32, jnp.where(sub == 0, y_low, roll(down, 1, 0)), down)
    upper_y = jnp.where(lane >= 96, jnp.where(sub == 7, y_high, roll(up, 7, 0)), up)
    z_low = roll(z_ghost[0, pl.ds(f * 8, 8)], 128 - x, 1)
    z_high = roll(z_ghost[1, pl.ds(f * 8, 8)], 31 - x + 128, 1)
    lower_z = jnp.where(lane % 32 == 0, z_low, roll(v, 1, 1))
    upper_z = jnp.where(lane % 32 == 31, z_high, roll(v, 127, 1))
    return v, (block[rows(at - pitch), :], block[rows(at + pitch), :], lower_y, upper_y, lower_z, upper_z)


def inside(block, fields, f, x):
    pitch = fields * 8
    lane, sub = iota(1), iota(0)
    at = (x + 1) * pitch + f * 8
    v = block[rows(at), :]
    down = roll(v, 32, 1)
    up = roll(v, 96, 1)
    lower_y = jnp.where(lane < 32, jnp.where(sub == 0, 0.0, roll(down, 1, 0)), down)
    upper_y = jnp.where(lane >= 96, jnp.where(sub == 7, 0.0, roll(up, 7, 0)), up)
    lower_z = jnp.where(lane % 32 == 0, 0.0, roll(v, 1, 1))
    upper_z = jnp.where(lane % 32 == 31, 0.0, roll(v, 127, 1))
    return v, (block[rows(at - pitch), :], block[rows(at + pitch), :], lower_y, upper_y, lower_z, upper_z)


def total(parts):
    return ((parts[0] + parts[1]) + (parts[2] + parts[3])) + (parts[4] + parts[5])


GROUPS = ((0, 1), (1, 3), (4, 3))
CHUNKS = 4
DIRECT = (0, 9)
MIXED = ()
PLAN = (
    ("arrange", 0),
    ("send", 0),
    ("arrange", 1),
    ("send", 1),
    ("arrange", 2),
    ("pack", 2),
    ("history", 0),
    ("interior", 1),
    ("collect", 0),
    ("begin", 0),
    ("send", 3),
    ("send", 4),
    ("send", 5),
    ("relay", 1),
    ("ship", 2),
    ("send", 6),
    ("relay", 3),
    ("relay", 4),
    ("species", 0),
    ("relay", 5),
    ("interior", 2),
    ("collect", 3),
    ("sweep", 0),
    ("send", 7),
    ("relay", 2),
    ("collect", 4),
    ("sweep", 1),
    ("send", 8),
    ("collect", 5),
    ("sweep", 2),
    ("send", 9),
    ("relay", 7),
    ("relay", 6),
    ("relay", 8),
    ("collect", 1),
    ("border", 1),
    ("collect", 2),
    ("border", 2),
    ("collect", 6),
    ("phase", 0),
    ("depart", 0),
    ("depart", 1),
    ("depart", 2),
    ("depart", 3),
    ("depart", 4),
    ("depart", 5),
    ("depart", 6),
    ("collect", 7),
    ("collect", 8),
    ("collect", 9),
)


def make_kernel(columns, devices):
    def kernel(state, new_slot_in, neighbor_in, stress_in, row_patch_in, *scratch):
        scratch = iter(scratch)

        def take(count):
            return [next(scratch) for _ in range(count)]

        second, y_last, z_last = take(3), take(3), take(3)
        weight, force, slope, base = take(4)
        (levels,) = take(1)
        send_e, stay_e, came_e = take(3), take(3), take(3)
        send_h, stay_h, came_h = take(3)
        cells = take(3)
        first = take(4)
        tables, y_ghosts, z_ghosts = take(10), take(7) + y_last, take(7) + z_last
        new_slot, neighbor, row_patch, stress = take(4)
        small_sem, load_sem, send_sem, recv_sem, face_send, face_recv = take(6)

        gz, xy = lax.axis_index("gz"), lax.axis_index("xy")
        device = gz * columns + xy
        left, right = device - 1, device + 1
        lower = (device - 1) * 2

        def place(d):
            return (d // columns, d % columns)

        loads = []
        for g, (low, count) in enumerate(GROUPS):
            part = pl.ds(low, count)
            loads.append(pltpu.make_async_copy(state.at[:, part], levels.at[:, part], load_sem.at[g]))
            loads[-1].start()

        small = []
        for k, (a, b) in enumerate(
            ((new_slot_in, new_slot), (neighbor_in, neighbor), (row_patch_in, row_patch), (stress_in, stress))
        ):
            small.append(pltpu.make_async_copy(a, b, small_sem.at[k]))
            small[-1].start()

        barrier = pltpu.get_barrier_semaphore()
        pl.semaphore_signal(barrier, inc=1, device_id=(1 - gz, xy), device_id_type=MESH)

        @pl.when(device > 0)
        def _():
            pl.semaphore_signal(barrier, inc=1, device_id=place(left), device_id_type=MESH)

        @pl.when(device < devices - 1)
        def _():
            pl.semaphore_signal(barrier, inc=1, device_id=place(right), device_id_type=MESH)

        @pl.when(device > 1)
        def _():
            pl.semaphore_signal(barrier, inc=1, device_id=place(device - 2), device_id_type=MESH)

        @pl.when(device < devices - 2)
        def _():
            pl.semaphore_signal(barrier, inc=1, device_id=place(device + 2), device_id_type=MESH)

        for copy in small:
            copy.wait()
        own = device * 2
        zero_stays = (new_slot[0] >= own) & (new_slot[0] < own + 2)
        stay_slot = jnp.where(zero_stays, new_slot[0], new_slot[1]) - own
        stays = [stay_slot == s for s in range(2)]

        sums = []
        for p in range(2):
            line = jnp.zeros((1, 128), jnp.float32)
            for r in range(stress.shape[0]):
                line = line + jnp.where(row_patch[r] == own + p, stress[r : r + 1, :], 0.0)
            sums.append(line)
        top = iota(0) == 0
        lines = pl.ds(EDGE * 8, 8)
        send_e[0][lines, :] = jnp.where(top, jnp.where(zero_stays, sums[1], sums[0]), 0.0)
        stay_e[0][lines, :] = jnp.where(top, jnp.where(zero_stays, sums[0], sums[1]), 0.0)

        def move(source, target, k):
            return pltpu.make_async_remote_copy(
                src_ref=source,
                dst_ref=target,
                send_sem=send_sem.at[k],
                recv_sem=recv_sem.at[k],
                device_id=(1 - gz, xy),
                device_id_type=MESH,
            )

        moves = [move(send_e[g], came_e[g], g) for g in range(3)] + [move(send_h, came_h, 3)]

        def combine_group(g):
            low, count = GROUPS[g]

            def combine(x, carry):
                for f in range(count):
                    to = rows((x * count + f) * 8)
                    to_h = rows((x * FIELDS + low + f) * 8)
                    both = []
                    for p in range(2):
                        part = pl.ds(x * 16 + p, 8, stride=2)
                        a, b, d = (levels.at[k, low + f][part, :] for k in range(3))
                        both.append(
                            (3.0 * a - 3.0 * b + d, (18.0 * a - 9.0 * b + 2.0 * d) * (1.0 / 11.0))
                        )
                    send_e[g][to, :] = jnp.where(zero_stays, both[1][0], both[0][0])
                    stay_e[g][to, :] = jnp.where(zero_stays, both[0][0], both[1][0])
                    send_h[to_h, :] = jnp.where(zero_stays, both[1][1], both[0][1])
                    stay_h[to_h, :] = jnp.where(zero_stays, both[0][1], both[1][1])
                return carry

            lax.fori_loop(0, EDGE, combine, 0, unroll=8 if count == 1 else 4)

        loads[0].wait()
        combine_group(0)
        below = (device + devices - 1) // devices + (device + devices - 2) // devices
        above = (2 * devices - 2 - device) // devices + (2 * devices - 3 - device) // devices
        pl.semaphore_wait(barrier, 1 + below + above)
        moves[0].start()
        for g in (1, 2):
            loads[g].wait()
            combine_group(g)
            moves[g].start()
        moves[3].start()

        def arrange_group(g):
            count = GROUPS[g][1]
            moves[g].wait_recv()

            def arrange(x, carry):
                part = pl.ds(pl.multiple_of(x * count * 8, 8), count * 8)
                to = pl.ds(pl.multiple_of((x + 1) * count * 8, 8), count * 8)
                here, there = stay_e[g][part, :], came_e[g][part, :]
                cells[g].at[0][to, :] = jnp.where(stays[0], here, there)
                cells[g].at[1][to, :] = jnp.where(stays[1], here, there)
                return carry

            lax.fori_loop(0, EDGE, arrange, 0, unroll=8 if count == 1 else 4)

        half = devices // 2
        odd = device % 2 == 1
        even = device % 2 == 0

        def send_to(k, which, source, to, target):
            return pltpu.make_async_remote_copy(
                src_ref=tables[k].at[pl.ds(source, 12)],
                dst_ref=tables[k].at[pl.ds(to, 12)],
                send_sem=face_send.at[3 * k + which],
                recv_sem=face_recv.at[3 * k + which],
                device_id=place(target),
                device_id_type=MESH,
            )

        def at(condition, act, *copy):
            @pl.when(condition)
            def _():
                act(send_to(*copy))

        def start(copy):
            copy.start()

        def arrive(copy):
            copy.wait_recv()

        def leave(copy):
            copy.wait_send()

        splits = [devices if k in DIRECT else half if k in MIXED else 0 for k in range(10)]

        def outward(k, act):
            split = splits[k]
            if split > 0:
                at(device < split - 1, act, k, 0, 12, 0, right)
                at((device > 0) & (device < split), act, k, 1, 12, 24, left)
            if 0 < split < devices:
                at(device == split - 1, act, k, 2, 12, 0, right)
                at(device == split, act, k, 2, 12, 24, left)
            if split < devices:
                at((device >= split) & even, act, k, 0, 12, 0, right)
                at((device >= split) & odd, act, k, 0, 12, 24, left)

        def onward(k, act):
            split = splits[k]
            if split < devices:
                at(even & (device >= split) & (device < devices - 2), act, k, 1, 24, 0, device + 2)
                at(odd & (device >= split + 2), act, k, 1, 0, 24, device - 2)

        def launch(k):
            outward(k, start)

        def hand_on(k):
            split = splits[k]
            if split < devices:
                at((device >= split) & even, arrive, k, 0, 12, 24, right)
                at((device >= split) & odd, arrive, k, 0, 12, 0, left)
                onward(k, start)

        def collect(k):
            split = splits[k]
            if split > 0:
                at((device < split) & (device > 0), arrive, k, 0, 12, 0, right)
                at(device < split - 1, arrive, k, 1, 12, 24, left)
            if 0 < split < devices:
                at(device == split - 1, arrive, k, 2, 12, 24, right)
                at(device == split, arrive, k, 2, 12, 0, left)
            if split < devices:
                at(even & (device > split), arrive, k, 1, 24, 0, left)
                at(odd & (device >= split) & (device < devices - 1), arrive, k, 1, 0, 24, right)
            fill_table(k)

        blocks = cells + first[:3] + [first[3]] + second
        widths = [1, 3, 3] + [1] * 7

        def pack_table(k):
            for s in range(2):
                pack(blocks[k].at[s], s, widths[k], tables[k], 0, widths[k])

        def fill_table(k):
            for s in range(2):
                fill(
                    blocks[k].at[s], s, widths[k], tables[k], neighbor, lower,
                    y_ghosts[k].at[s], z_ghosts[k].at[s], 0, widths[k],
                )

        def around(k, s, f, x):
            return nearby(blocks[k].at[s], widths[k], f, x, y_ghosts[k].at[s], z_ghosts[k].at[s])

        def begin(x, carry, traction):
            for s in range(2):
                v, near = around(0, s, 0, x)
                viscous = jnp.exp(0.3 * v)
                sides = [(viscous + jnp.exp(0.3 * n)) * 0.5 for n in near]
                inverse = 1.0 / (viscous + total(sides))
                half = 0.25 * v
                for i in range(6):
                    weight.at[s][rows((x * 6 + i) * 8), :] = sides[i] * inverse
                for k in range(3):
                    f = half * (near[2 * k + 1] - near[2 * k])
                    if k == 0:
                        f = f + jnp.where(x == 0, traction[s], 0.0)
                    f = f * inverse
                    force.at[s][rows((x * 3 + k) * 8), :] = f
                    first[k].at[s][rows((x + 1) * 8), :] = f
                laplace = total(near) - 6.0 * v
                first[3].at[s][rows((x + 1) * 8), :] = v * v * v - v - 0.5 * laplace
            return carry

        def species_step(g, within):
            low, count = GROUPS[g]

            def step(x, carry):
                for s in range(2):
                    if g > 0:
                        phi = cells[0].at[s][rows((x + 1) * 8), :]
                        biofilm = 0.5 * (1.0 + jnp.tanh(phi))
                    for f in range(low, low + count):
                        to = rows((x * 7 + f) * 8)
                        if within:
                            v, near = inside(cells[g].at[s], count, f - low, x)
                        else:
                            v, near = around(g, s, f - low, x)
                        for k in range(3):
                            slope.at[s][rows(((x * 7 + f) * 3 + k) * 8), :] = (
                                near[2 * k + 1] - near[2 * k]
                            ) * (0.5 * RATE)
                        history = jnp.where(stays[s], stay_h[to, :], came_h[to, :])
                        if f > 0:
                            laplace = total(near) - 6.0 * v
                            uptake = GROWTH[f - 1] * biofilm * v / (0.5 + jnp.abs(v))
                            history = history + RATE * (DIFFUSION[f - 1] * laplace - uptake)
                        base.at[s][to, :] = history
                return carry

            return step

        def species(g):
            lax.fori_loop(0, EDGE, species_step(g, False), 0, unroll=4)

        def interior(g):
            lax.fori_loop(1, EDGE - 1, species_step(g, True), 0, unroll=3)

        def border(g):
            low, count = GROUPS[g]
            full = species_step(g, False)
            full(0, 0)
            full(EDGE - 1, 0)
            lane, sub = iota(1), iota(0)
            y_first = (lane < 32) & (sub == 0)
            y_last = (lane >= 96) & (sub == 7)
            z_first, z_last = lane % 32 == 0, lane % 32 == 31

            def weights(first_mask, last_mask):
                c = 0.5 * RATE
                sign = jnp.where(first_mask, -c, jnp.where(last_mask, c, 0.0))
                return sign, jnp.where(first_mask | last_mask, RATE, 0.0)

            y_sign, y_weight = weights(y_first, y_last)
            z_sign, z_weight = weights(z_first, z_last)

            def fix(x, carry):
                for s in range(2):
                    yg, zg = y_ghosts[g].at[s], z_ghosts[g].at[s]
                    for f in range(count):
                        y = jnp.where(y_first, yg[0, pl.ds(f * 32 + x, 1)], yg[1, pl.ds(f * 32 + x, 1)])
                        z_low = roll(zg[0, pl.ds(f * 8, 8)], 128 - x, 1)
                        z_high = roll(zg[1, pl.ds(f * 8, 8)], 31 - x + 128, 1)
                        z = jnp.where(z_first, z_low, z_high)
                        to = (x * 7 + low + f) * 8
                        for k, part in ((1, y * y_sign), (2, z * z_sign)):
                            here = rows(to * 3 + k * 8)
                            slope.at[s][here, :] = slope.at[s][here, :] + part
                        here = rows(to)
                        part = DIFFUSION[low + f - 1] * (y * y_weight + z * z_weight)
                        base.at[s][here, :] = base.at[s][here, :] + part
                return carry

            lax.fori_loop(1, EDGE - 1, fix, 0, unroll=3)

        def sweep(c):
            def again(x, carry):
                for s in range(2):
                    near = around(3 + c, s, 0, x)[1]
                    second[c].at[s][rows((x + 1) * 8), :] = coupled(weight, force, near, c, s, x)
                return carry

            lax.fori_loop(0, EDGE, again, 0, unroll=16)

        def phase(x, carry):
            for s in range(2):
                v, near = around(6, s, 0, x)
                at = rows(x * 56)
                base.at[s][at, :] = base.at[s][at, :] + (0.2 * RATE) * (total(near) - 6.0 * v)
            return carry

        def depart(k):
            outward(k, leave)
            onward(k, leave)
            if k == 0:
                for copy in moves:
                    copy.wait_send()

        def flow():
            traction = [jnp.where(stays[s], stay_e[0][lines, :], came_e[0][lines, :]) for s in range(2)]
            lax.fori_loop(0, EDGE, lambda x, carry: begin(x, carry, traction), 0, unroll=4)

        acts = {
            "arrange": arrange_group,
            "pack": pack_table,
            "send": launch,
            "ship": launch,
            "depart": depart,
            "relay": hand_on,
            "collect": collect,
            "begin": lambda _: flow(),
            "sweep": sweep,
            "history": lambda _: moves[3].wait_recv(),
            "species": species,
            "interior": interior,
            "border": border,
            "phase": lambda _: lax.fori_loop(0, EDGE, phase, 0, unroll=4),
        }
        for act, which in PLAN:
            if act == "send":
                pack_table(which)
            acts[act](which)
        left_over = [k for k in range(10) if ("depart", k) not in PLAN]

        for k in left_over:
            depart(k)

    return kernel


def coupled(weight, force, near, c, s, x):
    sides = [weight.at[s][rows((x * 6 + i) * 8), :] for i in range(6)]
    return force.at[s][rows((x * 3 + c) * 8), :] + total([sides[i] * near[i] for i in range(6)])


def finish_kernel(*refs):
    second, y_last, z_last = refs[0:3], refs[3:6], refs[6:9]
    weight, force, slope, base, out_state, out_velocity, full_state, full_velocity, sem = refs[9:]
    width = EDGE * 16 // CHUNKS

    def stores(c):
        part = pl.ds(c * width, width)
        return (
            pltpu.make_async_copy(full_state.at[:, part], out_state.at[:, part], sem.at[2 * c]),
            pltpu.make_async_copy(full_velocity.at[:, part], out_velocity.at[:, part], sem.at[2 * c + 1]),
        )

    def finish(x, carry):
        for s in range(2):
            velocity = []
            for c in range(3):
                near = nearby(second[c].at[s], 1, 0, x, y_last[c].at[s], z_last[c].at[s])[1]
                velocity.append(coupled(weight, force, near, c, s, x))
            to = pl.ds(x * 16 + s, 8, stride=2)
            for k in range(3):
                full_velocity.at[k][to, :] = velocity[k]
            for f in range(FIELDS):
                advect = [velocity[k] * slope.at[s][rows(((x * 7 + f) * 3 + k) * 8), :] for k in range(3)]
                kept = base.at[s][rows((x * 7 + f) * 8), :]
                full_state.at[f][to, :] = kept - (advect[0] + advect[1] + advect[2])
        return carry

    def chunk(c, carry):
        planes = EDGE // CHUNKS
        lax.fori_loop(0, planes, lambda x, carry: finish(c * planes + x, carry), 0, unroll=4)
        for copy in stores(c):
            copy.start()
        return carry

    lax.fori_loop(0, CHUNKS, chunk, 0)
    for c in range(CHUNKS):
        for copy in stores(c):
            copy.wait()


def on_device(state, new_slot, neighbor, stress, row_patch):
    peers, columns = lax.axis_size("gz"), lax.axis_size("xy")
    assert peers == 2 and state.shape == (2, 3, FIELDS, CELLS)
    f32 = jnp.float32

    def vmem(*shape):
        return pltpu.VMEM(shape, f32)

    scratch = [vmem(3, FIELDS, EDGE * 16, 128)]
    for _ in range(3):
        scratch += [vmem(EDGE * 8 + 8, 128), vmem(EDGE * 24, 128), vmem(EDGE * 24, 128)]
    scratch += [vmem(EDGE * 56, 128)] * 3
    widths = (1, 3, 3) + (1,) * 7
    scratch += [vmem(2, 34 * c * 8, 128) for c in widths[:7]]
    scratch += [vmem(36, c * 8, 128) for c in widths]
    scratch += [vmem(2, 2, c * 32, 128) for c in widths[:7]]
    scratch += [vmem(2, 2, c * 8, 128) for c in widths[:7]]
    kept = [vmem(2, 34 * 8, 128)] * 3 + [vmem(2, 2, 32, 128)] * 3 + [vmem(2, 2, 8, 128)] * 3
    kept += [vmem(2, EDGE * n, 128) for n in (48, 24, 168, 56)]
    dma = pltpu.SemaphoreType.DMA
    small = ((new_slot, pltpu.SMEM), (neighbor, pltpu.SMEM), (row_patch, pltpu.SMEM), (stress, pltpu.VMEM))
    scratch += [space(a.shape, a.dtype) for a, space in small]
    scratch += [dma((n,)) for n in (4, 3, 4, 4, 30, 30)]
    woven = state.reshape(2, 3, FIELDS, EDGE * 8, 128).transpose(1, 2, 3, 0, 4)
    outs = pl.pallas_call(
        make_kernel(columns, peers * columns),
        out_shape=tuple(kept),
        in_specs=[pl.BlockSpec(memory_space=pltpu.HBM)] * 5,
        out_specs=(pl.BlockSpec(memory_space=pltpu.VMEM),) * len(kept),
        scratch_shapes=scratch,
        compiler_params=pltpu.CompilerParams(
            collective_id=0, has_side_effects=True, vmem_limit_bytes=36 * 2**20
        ),
    )(*(pltpu.with_memory_space_constraint(a, pltpu.HBM) for a in (woven.reshape(3, FIELDS, EDGE * 16, 128), new_slot, neighbor, stress, row_patch)))
    outs = pl.pallas_call(
        finish_kernel,
        out_shape=tuple(jax.ShapeDtypeStruct((n, EDGE * 16, 128), f32) for n in (FIELDS, 3)),
        in_specs=[pl.BlockSpec(memory_space=pltpu.VMEM)] * len(kept),
        out_specs=(pl.BlockSpec(memory_space=pltpu.HBM),) * 2,
        scratch_shapes=[vmem(FIELDS, EDGE * 16, 128), vmem(3, EDGE * 16, 128), dma((2 * CHUNKS,))],
        compiler_params=pltpu.CompilerParams(vmem_limit_bytes=16 * 2**20),
    )(*outs)
    return tuple(
        out.reshape(-1, EDGE * 8, 2, 128).transpose(2, 0, 1, 3).reshape(2, -1, CELLS) for out in outs
    )


def solution(mesh):
    both = ("gz", "xy")
    in_specs = (P(both, None, None, None), P(both), P(both, None), P(both, None), P(both))
    out_specs = (P(both, None, None), P(both, None, None))
    return jax.shard_map(
        on_device, mesh=mesh, in_specs=in_specs, out_specs=out_specs, check_vma=False
    )
```

```python
import jax
import jax.numpy as jnp
from jax import lax
from jax.experimental import pallas as pl
from jax.experimental.pallas import tpu as pltpu
from jax.sharding import PartitionSpec as P

EDGE = 32
CELLS = EDGE**3
FIELDS = 7
OPPOSITE = (1, 0, 3, 2, 5, 4)
DIFFUSION = (0.8, 1.0, 0.6, 1.2, 0.9, 0.7)
GROWTH = (1.0, 0.5, 2.0, 1.5, 0.8, 1.2)
RATE = 6.0 / 11.0 * 0.02
MESH = pl.DeviceIdType.MESH


def iota(axis):
    return lax.broadcasted_iota(jnp.int32, (8, 128), axis)


def roll(v, shift, axis):
    if isinstance(shift, int) and shift % v.shape[axis] == 0:
        return v
    if isinstance(shift, int):
        shift = shift % v.shape[axis]
    return pltpu.roll(v, shift, axis)


def rows(start):
    return pl.ds(start if isinstance(start, int) else pl.multiple_of(start, 8), 8)


def pack(block, slot, fields, table, first, count):
    pitch = fields * 8
    lane = iota(1)
    own = (2 + slot) * 6
    table[own] = block[pl.ds(pitch + first * 8, count * 8), :]
    table[own + 1] = block[pl.ds(EDGE * pitch + first * 8, count * 8), :]
    for f in range(count):
        low = high = None
        for j in range(4):
            at = (8 * j + 1) * pitch + (first + f) * 8
            a = roll(block[pl.ds(at, 8, stride=pitch), :], 32 * j, 1)
            b = roll(block[pl.ds(at + 7, 8, stride=pitch), :], 32 * j + 32, 1)
            low = a if j == 0 else jnp.where(lane // 32 == j, a, low)
            high = b if j == 0 else jnp.where(lane // 32 == j, b, high)
        table[own + 2, pl.ds(f * 8, 8)] = low
        table[own + 3, pl.ds(f * 8, 8)] = high

    for f in range(count):
        low = high = None
        for x in range(EDGE):
            v = roll(block[pl.ds((x + 1) * pitch + (first + f) * 8, 8), :], x, 1)
            low = v if x == 0 else jnp.where(lane % 32 == x, v, low)
            high = v if x == 0 else jnp.where(lane % 32 == x - 1, v, high)
        table[own + 4, pl.ds(f * 8, 8)] = low
        table[own + 5, pl.ds(f * 8, 8)] = roll(high, 97, 1)


def fill(block, slot, fields, table, neighbor, lower, y_ghost, z_ghost, first, count):
    pitch = fields * 8
    for face in range(6):
        beyond = neighbor[slot, face]
        inside = beyond >= 0
        pick = jnp.where(inside, jnp.clip(beyond - lower, 0, 5), 2) * 6 + OPPOSITE[face]
        tile = jnp.where(inside, table[pick], 0.0)
        if face == 0:
            block[pl.ds(first * 8, count * 8), :] = tile
        elif face == 1:
            block[pl.ds((EDGE + 1) * pitch + first * 8, count * 8), :] = tile
        elif face < 4:
            for f in range(count):
                one = tile[f * 8 : f * 8 + 8]
                for j in range(4):
                    shift = -32 * j if face == 2 else 96 - 32 * j
                    y_ghost[face - 2, pl.ds(f * 32 + j * 8, 8)] = roll(one, shift, 1)
        else:
            z_ghost[face - 4] = tile


def nearby(block, fields, f, x, y_ghost, z_ghost, first=0):
    pitch = fields * 8
    lane, sub = iota(1), iota(0)
    at = (x + 1) * pitch + f * 8
    v = block[rows(at), :]
    f = f - first
    y_low = y_ghost[0, pl.ds(f * 32 + x, 1)]
    y_high = y_ghost[1, pl.ds(f * 32 + x, 1)]
    down = roll(v, 32, 1)
    up = roll(v, 96, 1)
    lower_y = jnp.where(lane < 32, jnp.where(sub == 0, y_low, roll(down, 1, 0)), down)
    upper_y = jnp.where(lane >= 96, jnp.where(sub == 7, y_high, roll(up, 7, 0)), up)
    z_low = roll(z_ghost[0, pl.ds(f * 8, 8)], 128 - x, 1)
    z_high = roll(z_ghost[1, pl.ds(f * 8, 8)], 31 - x + 128, 1)
    lower_z = jnp.where(lane % 32 == 0, z_low, roll(v, 1, 1))
    upper_z = jnp.where(lane % 32 == 31, z_high, roll(v, 127, 1))
    return v, (block[rows(at - pitch), :], block[rows(at + pitch), :], lower_y, upper_y, lower_z, upper_z)


def inside(block, fields, f, x):
    pitch = fields * 8
    lane, sub = iota(1), iota(0)
    at = (x + 1) * pitch + f * 8
    v = block[rows(at), :]
    down = roll(v, 32, 1)
    up = roll(v, 96, 1)
    lower_y = jnp.where(lane < 32, jnp.where(sub == 0, 0.0, roll(down, 1, 0)), down)
    upper_y = jnp.where(lane >= 96, jnp.where(sub == 7, 0.0, roll(up, 7, 0)), up)
    lower_z = jnp.where(lane % 32 == 0, 0.0, roll(v, 1, 1))
    upper_z = jnp.where(lane % 32 == 31, 0.0, roll(v, 127, 1))
    return v, (block[rows(at - pitch), :], block[rows(at + pitch), :], lower_y, upper_y, lower_z, upper_z)


def total(parts):
    return ((parts[0] + parts[1]) + (parts[2] + parts[3])) + (parts[4] + parts[5])


GROUPS = ((0, 1), (1, 3), (4, 3))
CHUNKS = 4
DIRECT = (0, 9)
MIXED = ()
PLAN = (
    ("arrange", 0),
    ("send", 0),
    ("arrange", 1),
    ("send", 1),
    ("arrange", 2),
    ("pack", 2),
    ("history", 0),
    ("interior", 1),
    ("collect", 0),
    ("begin", 0),
    ("send", 3),
    ("send", 4),
    ("send", 5),
    ("relay", 1),
    ("ship", 2),
    ("send", 6),
    ("relay", 3),
    ("relay", 4),
    ("species", 0),
    ("relay", 5),
    ("interior", 2),
    ("collect", 3),
    ("sweep", 0),
    ("send", 7),
    ("relay", 2),
    ("collect", 4),
    ("sweep", 1),
    ("send", 8),
    ("collect", 5),
    ("sweep", 2),
    ("send", 9),
    ("relay", 7),
    ("last", 0),
    ("relay", 6),
    ("last", 1),
    ("relay", 8),
    ("last", 2),
    ("collect", 1),
    ("border", 1),
    ("collect", 2),
    ("border", 2),
    ("collect", 6),
    ("phase", 0),
    ("depart", 0),
    ("depart", 1),
    ("depart", 2),
    ("depart", 3),
    ("depart", 4),
    ("depart", 5),
    ("depart", 6),
    ("collect", 7),
    ("rim", 0),
    ("collect", 8),
    ("rim", 1),
    ("collect", 9),
    ("rim", 2),
)


def make_kernel(columns, devices):
    def kernel(state, new_slot_in, neighbor_in, stress_in, row_patch_in, *scratch):
        scratch = iter(scratch)

        def take(count):
            return [next(scratch) for _ in range(count)]

        ahead, y_last, z_last = take(3), take(3), take(3)
        weight, slope, base = take(3)
        (levels, force) = take(2)
        send_e, stay_e, came_e = take(3), take(3), take(3)
        send_h, stay_h, came_h = take(3)
        cells = take(3)
        first, second = take(4), take(3)
        tables, y_ghosts, z_ghosts = take(10), take(7) + y_last, take(7) + z_last
        new_slot, neighbor, row_patch, stress = take(4)
        small_sem, load_sem, send_sem, recv_sem, face_send, face_recv = take(6)

        gz, xy = lax.axis_index("gz"), lax.axis_index("xy")
        device = gz * columns + xy
        left, right = device - 1, device + 1
        lower = (device - 1) * 2

        def place(d):
            return (d // columns, d % columns)

        loads = []
        for g, (low, count) in enumerate(GROUPS):
            part = pl.ds(low, count)
            loads.append(pltpu.make_async_copy(state.at[:, part], levels.at[:, part], load_sem.at[g]))
            loads[-1].start()

        small = []
        for k, (a, b) in enumerate(
            ((new_slot_in, new_slot), (neighbor_in, neighbor), (row_patch_in, row_patch), (stress_in, stress))
        ):
            small.append(pltpu.make_async_copy(a, b, small_sem.at[k]))
            small[-1].start()

        barrier = pltpu.get_barrier_semaphore()
        pl.semaphore_signal(barrier, inc=1, device_id=(1 - gz, xy), device_id_type=MESH)

        @pl.when(device > 0)
        def _():
            pl.semaphore_signal(barrier, inc=1, device_id=place(left), device_id_type=MESH)

        @pl.when(device < devices - 1)
        def _():
            pl.semaphore_signal(barrier, inc=1, device_id=place(right), device_id_type=MESH)

        @pl.when(device > 1)
        def _():
            pl.semaphore_signal(barrier, inc=1, device_id=place(device - 2), device_id_type=MESH)

        @pl.when(device < devices - 2)
        def _():
            pl.semaphore_signal(barrier, inc=1, device_id=place(device + 2), device_id_type=MESH)

        for copy in small:
            copy.wait()
        own = device * 2
        zero_stays = (new_slot[0] >= own) & (new_slot[0] < own + 2)
        stay_slot = jnp.where(zero_stays, new_slot[0], new_slot[1]) - own
        stays = [stay_slot == s for s in range(2)]

        sums = []
        for p in range(2):
            line = jnp.zeros((1, 128), jnp.float32)
            for r in range(stress.shape[0]):
                line = line + jnp.where(row_patch[r] == own + p, stress[r : r + 1, :], 0.0)
            sums.append(line)
        top = iota(0) == 0
        lines = pl.ds(EDGE * 8, 8)
        send_e[0][lines, :] = jnp.where(top, jnp.where(zero_stays, sums[1], sums[0]), 0.0)
        stay_e[0][lines, :] = jnp.where(top, jnp.where(zero_stays, sums[0], sums[1]), 0.0)

        def move(source, target, k):
            return pltpu.make_async_remote_copy(
                src_ref=source,
                dst_ref=target,
                send_sem=send_sem.at[k],
                recv_sem=recv_sem.at[k],
                device_id=(1 - gz, xy),
                device_id_type=MESH,
            )

        moves = [move(send_e[g], came_e[g], g) for g in range(3)] + [move(send_h, came_h, 3)]

        def combine_group(g):
            low, count = GROUPS[g]

            def combine(x, carry):
                for f in range(count):
                    to = rows((x * count + f) * 8)
                    to_h = rows((x * FIELDS + low + f) * 8)
                    both = []
                    for p in range(2):
                        part = pl.ds(x * 16 + p, 8, stride=2)
                        a, b, d = (levels.at[k, low + f][part, :] for k in range(3))
                        both.append(
                            (3.0 * a - 3.0 * b + d, (18.0 * a - 9.0 * b + 2.0 * d) * (1.0 / 11.0))
                        )
                    send_e[g][to, :] = jnp.where(zero_stays, both[1][0], both[0][0])
                    stay_e[g][to, :] = jnp.where(zero_stays, both[0][0], both[1][0])
                    send_h[to_h, :] = jnp.where(zero_stays, both[1][1], both[0][1])
                    stay_h[to_h, :] = jnp.where(zero_stays, both[0][1], both[1][1])
                return carry

            lax.fori_loop(0, EDGE, combine, 0, unroll=8 if count == 1 else 4)

        loads[0].wait()
        combine_group(0)
        below = (device + devices - 1) // devices + (device + devices - 2) // devices
        above = (2 * devices - 2 - device) // devices + (2 * devices - 3 - device) // devices
        pl.semaphore_wait(barrier, 1 + below + above)
        moves[0].start()
        for g in (1, 2):
            loads[g].wait()
            combine_group(g)
            moves[g].start()
        moves[3].start()

        def arrange_group(g):
            count = GROUPS[g][1]
            moves[g].wait_recv()

            def arrange(x, carry):
                part = pl.ds(pl.multiple_of(x * count * 8, 8), count * 8)
                to = pl.ds(pl.multiple_of((x + 1) * count * 8, 8), count * 8)
                here, there = stay_e[g][part, :], came_e[g][part, :]
                cells[g].at[0][to, :] = jnp.where(stays[0], here, there)
                cells[g].at[1][to, :] = jnp.where(stays[1], here, there)
                return carry

            lax.fori_loop(0, EDGE, arrange, 0, unroll=8 if count == 1 else 4)

        half = devices // 2
        odd = device % 2 == 1
        even = device % 2 == 0

        def send_to(k, which, source, to, target):
            return pltpu.make_async_remote_copy(
                src_ref=tables[k].at[pl.ds(source, 12)],
                dst_ref=tables[k].at[pl.ds(to, 12)],
                send_sem=face_send.at[3 * k + which],
                recv_sem=face_recv.at[3 * k + which],
                device_id=place(target),
                device_id_type=MESH,
            )

        def at(condition, act, *copy):
            @pl.when(condition)
            def _():
                act(send_to(*copy))

        def start(copy):
            copy.start()

        def arrive(copy):
            copy.wait_recv()

        def leave(copy):
            copy.wait_send()

        splits = [devices if k in DIRECT else half if k in MIXED else 0 for k in range(10)]

        def outward(k, act):
            split = splits[k]
            if split > 0:
                at(device < split - 1, act, k, 0, 12, 0, right)
                at((device > 0) & (device < split), act, k, 1, 12, 24, left)
            if 0 < split < devices:
                at(device == split - 1, act, k, 2, 12, 0, right)
                at(device == split, act, k, 2, 12, 24, left)
            if split < devices:
                at((device >= split) & even, act, k, 0, 12, 0, right)
                at((device >= split) & odd, act, k, 0, 12, 24, left)

        def onward(k, act):
            split = splits[k]
            if split < devices:
                at(even & (device >= split) & (device < devices - 2), act, k, 1, 24, 0, device + 2)
                at(odd & (device >= split + 2), act, k, 1, 0, 24, device - 2)

        def launch(k):
            outward(k, start)

        def hand_on(k):
            split = splits[k]
            if split < devices:
                at((device >= split) & even, arrive, k, 0, 12, 24, right)
                at((device >= split) & odd, arrive, k, 0, 12, 0, left)
                onward(k, start)

        def collect(k):
            split = splits[k]
            if split > 0:
                at((device < split) & (device > 0), arrive, k, 0, 12, 0, right)
                at(device < split - 1, arrive, k, 1, 12, 24, left)
            if 0 < split < devices:
                at(device == split - 1, arrive, k, 2, 12, 24, right)
                at(device == split, arrive, k, 2, 12, 0, left)
            if split < devices:
                at(even & (device > split), arrive, k, 1, 24, 0, left)
                at(odd & (device >= split) & (device < devices - 1), arrive, k, 1, 0, 24, right)
            fill_table(k)

        blocks = cells + first[:3] + [first[3]] + second
        widths = [1, 3, 3] + [1] * 7

        def pack_table(k):
            for s in range(2):
                pack(blocks[k].at[s], s, widths[k], tables[k], 0, widths[k])

        def fill_table(k):
            for s in range(2):
                fill(
                    blocks[k].at[s], s, widths[k], tables[k], neighbor, lower,
                    y_ghosts[k].at[s], z_ghosts[k].at[s], 0, widths[k],
                )

        def around(k, s, f, x):
            return nearby(blocks[k].at[s], widths[k], f, x, y_ghosts[k].at[s], z_ghosts[k].at[s])

        def begin(x, carry, traction):
            for s in range(2):
                v, near = around(0, s, 0, x)
                viscous = jnp.exp(0.3 * v)
                sides = [(viscous + jnp.exp(0.3 * n)) * 0.5 for n in near]
                inverse = 1.0 / (viscous + total(sides))
                half = 0.25 * v
                for i in range(6):
                    weight.at[s][rows((x * 6 + i) * 8), :] = sides[i] * inverse
                for k in range(3):
                    f = half * (near[2 * k + 1] - near[2 * k])
                    if k == 0:
                        f = f + jnp.where(x == 0, traction[s], 0.0)
                    f = f * inverse
                    force.at[s][rows((x * 3 + k) * 8), :] = f
                    first[k].at[s][rows((x + 1) * 8), :] = f
                laplace = total(near) - 6.0 * v
                first[3].at[s][rows((x + 1) * 8), :] = v * v * v - v - 0.5 * laplace
            return carry

        def species_step(g, within):
            low, count = GROUPS[g]

            def step(x, carry):
                for s in range(2):
                    if g > 0:
                        phi = cells[0].at[s][rows((x + 1) * 8), :]
                        biofilm = 0.5 * (1.0 + jnp.tanh(phi))
                    for f in range(low, low + count):
                        to = rows((x * 7 + f) * 8)
                        if within:
                            v, near = inside(cells[g].at[s], count, f - low, x)
                        else:
                            v, near = around(g, s, f - low, x)
                        for k in range(3):
                            slope.at[s][rows(((x * 7 + f) * 3 + k) * 8), :] = (
                                near[2 * k + 1] - near[2 * k]
                            ) * (0.5 * RATE)
                        history = jnp.where(stays[s], stay_h[to, :], came_h[to, :])
                        if f > 0:
                            laplace = total(near) - 6.0 * v
                            uptake = GROWTH[f - 1] * biofilm * v / (0.5 + jnp.abs(v))
                            history = history + RATE * (DIFFUSION[f - 1] * laplace - uptake)
                        base.at[s][to, :] = history
                return carry

            return step

        def species(g):
            lax.fori_loop(0, EDGE, species_step(g, False), 0, unroll=4)

        def interior(g):
            lax.fori_loop(1, EDGE - 1, species_step(g, True), 0, unroll=5)

        def border(g):
            low, count = GROUPS[g]
            full = species_step(g, False)
            full(0, 0)
            full(EDGE - 1, 0)
            lane, sub = iota(1), iota(0)
            y_first = (lane < 32) & (sub == 0)
            y_last = (lane >= 96) & (sub == 7)
            z_first, z_last = lane % 32 == 0, lane % 32 == 31

            def weights(first_mask, last_mask):
                c = 0.5 * RATE
                sign = jnp.where(first_mask, -c, jnp.where(last_mask, c, 0.0))
                return sign, jnp.where(first_mask | last_mask, RATE, 0.0)

            y_sign, y_weight = weights(y_first, y_last)
            z_sign, z_weight = weights(z_first, z_last)

            def fix(x, carry):
                for s in range(2):
                    yg, zg = y_ghosts[g].at[s], z_ghosts[g].at[s]
                    for f in range(count):
                        y = jnp.where(y_first, yg[0, pl.ds(f * 32 + x, 1)], yg[1, pl.ds(f * 32 + x, 1)])
                        z_low = roll(zg[0, pl.ds(f * 8, 8)], 128 - x, 1)
                        z_high = roll(zg[1, pl.ds(f * 8, 8)], 31 - x + 128, 1)
                        z = jnp.where(z_first, z_low, z_high)
                        to = (x * 7 + low + f) * 8
                        for k, part in ((1, y * y_sign), (2, z * z_sign)):
                            here = rows(to * 3 + k * 8)
                            slope.at[s][here, :] = slope.at[s][here, :] + part
                        here = rows(to)
                        part = DIFFUSION[low + f - 1] * (y * y_weight + z * z_weight)
                        base.at[s][here, :] = base.at[s][here, :] + part
                return carry

            lax.fori_loop(1, EDGE - 1, fix, 0, unroll=3)

        def planes_within(k, c, target):
            def planes(x, carry):
                for s in range(2):
                    near = inside(blocks[k].at[s], 1, 0, x)[1]
                    target.at[s][rows(x * 8), :] = coupled(weight, force, near, c, s, x)
                return carry

            return planes

        def whole_planes(c):
            def planes(x, carry):
                for s in range(2):
                    near = around(3 + c, s, 0, x)[1]
                    second[c].at[s][rows((x + 1) * 8), :] = coupled(weight, force, near, c, s, x)
                return carry

            return planes

        def sweep(c):
            lax.fori_loop(0, EDGE, whole_planes(c), 0, unroll=16)

        def last(c):
            lax.fori_loop(1, EDGE - 1, planes_within(7 + c, c, ahead[c]), 0, unroll=10)

        def rim(c):
            for x in (0, EDGE - 1):
                planes_within(7 + c, c, ahead[c])(x, 0)

        def phase(x, carry):
            for s in range(2):
                v, near = around(6, s, 0, x)
                at = rows(x * 56)
                base.at[s][at, :] = base.at[s][at, :] + (0.2 * RATE) * (total(near) - 6.0 * v)
            return carry

        def depart(k):
            outward(k, leave)
            onward(k, leave)
            if k == 0:
                for copy in moves:
                    copy.wait_send()

        def flow():
            traction = [jnp.where(stays[s], stay_e[0][lines, :], came_e[0][lines, :]) for s in range(2)]
            lax.fori_loop(0, EDGE, lambda x, carry: begin(x, carry, traction), 0, unroll=8)

        acts = {
            "arrange": arrange_group,
            "pack": pack_table,
            "send": launch,
            "ship": launch,
            "depart": depart,
            "relay": hand_on,
            "collect": collect,
            "begin": lambda _: flow(),
            "sweep": sweep,
            "last": last,
            "rim": rim,
            "history": lambda _: moves[3].wait_recv(),
            "species": species,
            "interior": interior,
            "border": border,
            "phase": lambda _: lax.fori_loop(0, EDGE, phase, 0, unroll=4),
        }
        for act, which in PLAN:
            if act == "send":
                pack_table(which)
            acts[act](which)
        left_over = [k for k in range(10) if ("depart", k) not in PLAN]

        for k in left_over:
            depart(k)

    return kernel


def beyond_terms(weight, y_ghost, z_ghost, s, x):
    lane, sub = iota(1), iota(0)
    y_first, y_last = (lane < 32) & (sub == 0), (lane >= 96) & (sub == 7)
    z_first, z_last = lane % 32 == 0, lane % 32 == 31
    sides = [weight.at[s][rows((x * 6 + i) * 8), :] for i in range(2, 6)]
    y = jnp.where(y_first, y_ghost[0, pl.ds(x, 1)], y_ghost[1, pl.ds(x, 1)])
    z_low = roll(z_ghost[0], 128 - x, 1)
    z_high = roll(z_ghost[1], 31 - x + 128, 1)
    z = jnp.where(z_first, z_low, z_high)
    y_side = jnp.where(y_first, sides[0], jnp.where(y_last, sides[1], 0.0))
    z_side = jnp.where(z_first, sides[2], jnp.where(z_last, sides[3], 0.0))
    return y * y_side + z * z_side


def coupled(weight, force, near, c, s, x):
    sides = [weight.at[s][rows((x * 6 + i) * 8), :] for i in range(6)]
    return force.at[s][rows((x * 3 + c) * 8), :] + total([sides[i] * near[i] for i in range(6)])


def finish_kernel(*refs):
    ahead, y_last, z_last = refs[0:3], refs[3:6], refs[6:9]
    weight, slope, base, out_state, out_velocity, full_state, full_velocity, sem = refs[9:]
    width = EDGE * 16 // CHUNKS

    def stores(c):
        part = pl.ds(c * width, width)
        return (
            pltpu.make_async_copy(full_state.at[:, part], out_state.at[:, part], sem.at[2 * c]),
            pltpu.make_async_copy(full_velocity.at[:, part], out_velocity.at[:, part], sem.at[2 * c + 1]),
        )

    def finish(x, carry):
        for s in range(2):
            velocity = []
            for c in range(3):
                part = beyond_terms(weight, y_last[c].at[s], z_last[c].at[s], s, x)
                velocity.append(ahead[c].at[s][rows(x * 8), :] + part)
            to = pl.ds(x * 16 + s, 8, stride=2)
            for k in range(3):
                full_velocity.at[k][to, :] = velocity[k]
            for f in range(FIELDS):
                advect = [velocity[k] * slope.at[s][rows(((x * 7 + f) * 3 + k) * 8), :] for k in range(3)]
                kept = base.at[s][rows((x * 7 + f) * 8), :]
                full_state.at[f][to, :] = kept - (advect[0] + advect[1] + advect[2])
        return carry

    def chunk(c, carry):
        planes = EDGE // CHUNKS
        lax.fori_loop(0, planes, lambda x, carry: finish(c * planes + x, carry), 0, unroll=8)
        for copy in stores(c):
            copy.start()
        return carry

    lax.fori_loop(0, CHUNKS, chunk, 0)
    for c in range(CHUNKS):
        for copy in stores(c):
            copy.wait()


def on_device(state, new_slot, neighbor, stress, row_patch):
    peers, columns = lax.axis_size("gz"), lax.axis_size("xy")
    assert peers == 2 and state.shape == (2, 3, FIELDS, CELLS)
    f32 = jnp.float32

    def vmem(*shape):
        return pltpu.VMEM(shape, f32)

    scratch = [vmem(3, FIELDS, EDGE * 16, 128), vmem(2, EDGE * 24, 128)]
    for _ in range(3):
        scratch += [vmem(EDGE * 8 + 8, 128), vmem(EDGE * 24, 128), vmem(EDGE * 24, 128)]
    scratch += [vmem(EDGE * 56, 128)] * 3
    widths = (1, 3, 3) + (1,) * 7
    scratch += [vmem(2, 34 * c * 8, 128) for c in widths[:7] + (1,) * 3]
    scratch += [vmem(36, c * 8, 128) for c in widths]
    scratch += [vmem(2, 2, c * 32, 128) for c in widths[:7]]
    scratch += [vmem(2, 2, c * 8, 128) for c in widths[:7]]
    kept = [vmem(2, EDGE * 8, 128)] * 3 + [vmem(2, 2, 32, 128)] * 3 + [vmem(2, 2, 8, 128)] * 3
    kept += [vmem(2, EDGE * n, 128) for n in (48, 168, 56)]
    dma = pltpu.SemaphoreType.DMA
    small = ((new_slot, pltpu.SMEM), (neighbor, pltpu.SMEM), (row_patch, pltpu.SMEM), (stress, pltpu.VMEM))
    scratch += [space(a.shape, a.dtype) for a, space in small]
    scratch += [dma((n,)) for n in (4, 3, 4, 4, 30, 30)]
    woven = state.reshape(2, 3, FIELDS, EDGE * 8, 128).transpose(1, 2, 3, 0, 4)
    outs = pl.pallas_call(
        make_kernel(columns, peers * columns),
        out_shape=tuple(kept),
        in_specs=[pl.BlockSpec(memory_space=pltpu.HBM)] * 5,
        out_specs=(pl.BlockSpec(memory_space=pltpu.VMEM),) * len(kept),
        scratch_shapes=scratch,
        compiler_params=pltpu.CompilerParams(
            collective_id=0, has_side_effects=True, vmem_limit_bytes=36 * 2**20
        ),
    )(*(pltpu.with_memory_space_constraint(a, pltpu.HBM) for a in (woven.reshape(3, FIELDS, EDGE * 16, 128), new_slot, neighbor, stress, row_patch)))
    outs = pl.pallas_call(
        finish_kernel,
        out_shape=tuple(jax.ShapeDtypeStruct((n, EDGE * 16, 128), f32) for n in (FIELDS, 3)),
        in_specs=[pl.BlockSpec(memory_space=pltpu.VMEM)] * len(kept),
        out_specs=(pl.BlockSpec(memory_space=pltpu.HBM),) * 2,
        scratch_shapes=[vmem(FIELDS, EDGE * 16, 128), vmem(3, EDGE * 16, 128), dma((2 * CHUNKS,))],
        compiler_params=pltpu.CompilerParams(vmem_limit_bytes=16 * 2**20),
    )(*outs)
    return tuple(
        out.reshape(-1, EDGE * 8, 2, 128).transpose(2, 0, 1, 3).reshape(2, -1, CELLS) for out in outs
    )


def solution(mesh):
    both = ("gz", "xy")
    in_specs = (P(both, None, None, None), P(both), P(both, None), P(both, None), P(both))
    out_specs = (P(both, None, None), P(both, None, None))
    return jax.shard_map(
        on_device, mesh=mesh, in_specs=in_specs, out_specs=out_specs, check_vma=False
    )
```
